32 devices in a mesh: dp: 8 (over z, x), tensor: 4 (over y, core).
Axes of the slice: x: 2, y: 2, z: 4, core: 2. Of those that a mesh axis runs over, the one named last changes fastest.
Arguments:
- inputs: bfloat16 [16384, 768], P(('dp', 'tensor')), may hold values from -6 to 6
- teacher: bfloat16 [16384, 768], P(('dp', 'tensor')), may hold values from -6 to 6
- lengths: int32 [8], P('dp'), may hold values from 512 to 2048
- buckets: int32 [4096], replicated, may hold values from 0 to 31
- gain_attn: bfloat16 [768], replicated, may hold values from 0.25 to 1.75
- w_query: bfloat16 [768, 768], P(None, 'tensor'), may hold values from -0.4375 to 0.4375
- w_key: bfloat16 [768, 768], P(None, 'tensor'), may hold values from -0.21875 to 0.21875
- w_value: bfloat16 [768, 768], P(None, 'tensor'), may hold values from -0.21875 to 0.21875
- w_out: bfloat16 [768, 768], P('tensor'), may hold values from -1.75 to 1.75
- bias_table: bfloat16 [32, 12], P(None, 'tensor'), may hold values from -4 to 4
- gain_ff: bfloat16 [768], replicated, may hold values from 0.25 to 1.75
- w_gate: bfloat16 [768, 2048], P(None, 'tensor'), may hold values from -0.21875 to 0.21875
- w_up: bfloat16 [768, 2048], P(None, 'tensor'), may hold values from -0.21875 to 0.21875
- w_down: bfloat16 [2048, 768], P('tensor'), may hold values from -0.125 to 0.125
Outputs:
- activations: bfloat16 [16384, 768], P(('dp', 'tensor'))
- loss: float32 [], replicated
- grad_inputs: float32 [16384, 768], P(('dp', 'tensor'))
- grad_gain_attn: float32 [768], replicated
- grad_query: float32 [768, 768], P(None, 'tensor')
- grad_key: float32 [768, 768], P(None, 'tensor')
- grad_value: float32 [768, 768], P(None, 'tensor')
- grad_out: float32 [768, 768], P('tensor')
- grad_table: float32 [32, 12], P(None, 'tensor')
- grad_gain_ff: float32 [768], replicated
- grad_gate: float32 [768, 2048], P(None, 'tensor')
- grad_up: float32 [768, 2048], P(None, 'tensor')
- grad_down: float32 [2048, 768], P('tensor')
The draws below stay inside these ranges and needn't reach their ends.
All inputs are finite; a program needn't handle non-finite values.
Results may differ from the reference program's by a relative error of at most 0.015.
The reference program's roundings to bfloat16 on the way count: a program that leaves them out, or rounds other values in their place, can miss the bound.
Values may be sent and summed in bfloat16 or wider, within the bound.
A program may use at most 320 MiB of HBM per device.

```python
import jax
import jax.numpy as jnp
from jax import lax

D = 768
HEADS = 12
HEAD_DIM = 64
FF = 2048
BUCKETS = 32
SEQ_LEN = 2048
SEQS = 8
TOKENS = 16384


def touch_ends(values, own_key, smallest, largest):
    longest = values.shape.index(max(values.shape))
    spots = []
    for shift in (0, 1):
        where = [jax.random.randint(jax.random.fold_in(own_key, axis), (), 0, length) for axis, length in enumerate(values.shape)]
        where[longest] = (where[longest] + shift) % values.shape[longest]
        spots.append(tuple(where))
    return values.at[spots[0]].set(smallest).at[spots[1]].set(largest)


def shard_levels(key, dims, split, least, largest):
    level, own = 1.0, jax.random.fold_in(key, 6)
    for axis_at, blocks in split:
        steps = jnp.exp(jax.random.uniform(jax.random.fold_in(own, axis_at), (blocks,), jnp.float32, least / len(split), largest / len(split)))
        level = level * jnp.repeat(steps, dims[axis_at] // blocks).reshape([-1 if axis == axis_at else 1 for axis in range(len(dims))])
    return level


def normal_values(rng, dims, spread, most, pieces=(), held_as=jnp.bfloat16):
    level = shard_levels(rng, dims, pieces, -0.22, 0.18) if pieces else 1.0
    array = jax.random.normal(rng, dims, jnp.float32) * spread * level
    return jnp.minimum(jnp.maximum(array, -most), most).astype(held_as)


def setup_inputs(seed: int = 0) -> dict:
    key_list = jax.random.split(jax.random.key(seed), 15)
    return {
        "inputs": normal_values(key_list[0], (TOKENS, D), 1.0, 6.0, ((0, 32),)),
        "teacher": normal_values(key_list[1], (TOKENS, D), 1.0, 6.0, ((0, 32),)),
        "lengths": touch_ends(jax.random.randint(key_list[2], (SEQS,), SEQ_LEN // 4, SEQ_LEN + 1), jax.random.fold_in(key_list[2], 1), SEQ_LEN // 4, SEQ_LEN).astype(jnp.int32),
        "buckets": touch_ends(jax.random.randint(key_list[3], (2 * SEQ_LEN,), 0, BUCKETS), jax.random.fold_in(key_list[3], 1), 0, BUCKETS - 1).astype(jnp.int32),
        "gain_attn": jnp.clip(1.0 + 0.15 * jax.random.normal(key_list[4], (D,), jnp.float32), 0.25, 1.75).astype(jnp.bfloat16),
        "w_query": normal_values(key_list[5], (D, D), (D // 4) ** -0.5, 0.4375, ((1, 4),)),
        "w_key": normal_values(key_list[6], (D, D), D ** -0.5, 0.21875, ((1, 4),)),
        "w_value": normal_values(key_list[7], (D, D), D ** -0.5, 0.21875, ((1, 4),)),
        "w_out": normal_values(key_list[8], (D, D), (max(D // 64, 4)) ** -0.5, 1.75, ((0, 4),)),
        "bias_table": normal_values(key_list[9], (BUCKETS, HEADS), 1.0, 4.0, ((1, 4),)),
        "gain_ff": jnp.clip(1.0 + 0.15 * jax.random.normal(key_list[10], (D,), jnp.float32), 0.25, 1.75).astype(jnp.bfloat16),
        "w_gate": normal_values(key_list[11], (D, FF), D ** -0.5, 0.21875, ((1, 4),)),
        "w_up": normal_values(key_list[12], (D, FF), D ** -0.5, 0.21875, ((1, 4),)),
        "w_down": normal_values(key_list[13], (FF, D), FF ** -0.5, 0.125, ((0, 4),)),
    }


@jax.custom_vjp
def low(v):
    return lax.optimization_barrier(v.astype(jnp.bfloat16)).astype(jnp.float32)

@jax.custom_vjp
def low_back(v):
    return v

def low_keep(v):
    return (low(v), None)

def low_pass(kept, grad):
    return (grad,)

def back_keep(v):
    return (v, None)

def back_low(kept, grad):
    return (low(grad),)
low.defvjp(low_keep, low_pass)
low_back.defvjp(back_keep, back_low)
eps_norm = 1e-06
masked_score = -1e+30
highest = lax.Precision.HIGHEST

def row_norm(values, gain):
    inverse = lax.rsqrt(lax.optimization_barrier(jnp.mean(values * values, axis=-1, keepdims=True)) + eps_norm)
    return values * inverse * gain

def both_ways(values):
    return low(low_back(values))

def attend(query_seq, key_seq, value_seq, keep_seq, length, relative):
    places = jnp.arange(SEQ_LEN, dtype=jnp.int32)
    offsets = places[None, :] - places[:, None] + SEQ_LEN
    bias_rows = relative[:, offsets]
    raw_scores = jnp.einsum('qhd,khd->hqk', query_seq, key_seq, precision=highest) * HEAD_DIM ** (-0.5)
    scores = low_back(raw_scores + bias_rows)
    scores = jnp.where((places < length)[None, None, :], scores, masked_score)
    probs = low(jax.nn.softmax(scores, axis=-1))
    mixed = jnp.einsum('hqk,khd->qhd', probs, value_seq, precision=highest).reshape(SEQ_LEN, D)
    return both_ways(mixed * keep_seq[:, None])

def reference(inputs, teacher, lengths, buckets, gain_attn, w_query, w_key, w_value, w_out, bias_table, gain_ff, w_gate, w_up, w_down):
    places = jnp.arange(TOKENS, dtype=jnp.int32)
    keep_mask = (places % SEQ_LEN < lengths[places // SEQ_LEN]).astype(jnp.float32)

    def forward(source, gain_a, weight_q, weight_k, weight_v, weight_o, table, gain_f, weight_g, weight_u, weight_d):
        normed = low(row_norm(source, gain_a))
        query = both_ways(jnp.dot(normed, weight_q, precision=highest)).reshape(SEQS, SEQ_LEN, HEADS, HEAD_DIM)
        key = both_ways(jnp.dot(normed, weight_k, precision=highest)).reshape(SEQS, SEQ_LEN, HEADS, HEAD_DIM)
        value = both_ways(jnp.dot(normed, weight_v, precision=highest)).reshape(SEQS, SEQ_LEN, HEADS, HEAD_DIM)
        relative = table[buckets].T
        attend_saved = jax.checkpoint(attend)
        mixed = lax.map(lambda items: attend_saved(items[0], items[1], items[2], items[3], items[4], relative), (query, key, value, keep_mask.reshape(SEQS, SEQ_LEN), lengths)).reshape(TOKENS, D)
        middle = source + low_back(jnp.dot(mixed, weight_o, precision=highest))
        normed_ff = low(row_norm(middle, gain_f))
        gate_values = low_back(jnp.dot(normed_ff, weight_g, precision=highest))
        up_values = low_back(jnp.dot(normed_ff, weight_u, precision=highest))
        hidden = low(keep_mask[:, None] * jax.nn.gelu(gate_values, approximate=True) * up_values)
        return middle + low_back(jnp.dot(hidden, weight_d, precision=highest))
    floats = (inputs, gain_attn, w_query, w_key, w_value, w_out, bias_table, gain_ff, w_gate, w_up, w_down)
    floats = tuple((item.astype(jnp.float32) for item in floats))
    output, backward = jax.vjp(forward, *floats)
    cotangent = keep_mask[:, None] * (output - teacher.astype(jnp.float32))
    grads = backward(cotangent)
    count = jnp.sum(keep_mask)
    scale = 2.0 / (count * D)
    loss = jnp.sum(cotangent * cotangent) / (count * D)
    return (output.astype(jnp.bfloat16), loss, grads[0] * scale, grads[1] * scale, grads[2] * scale, grads[3] * scale, grads[4] * scale, grads[5] * scale, grads[6] * scale, grads[7] * scale, grads[8] * scale, grads[9] * scale, grads[10] * scale)
```

```python
import jax
import jax.numpy as jnp
from jax import lax
from jax.experimental import pallas as pl
from jax.experimental.pallas import tpu as pltpu
from jax.sharding import PartitionSpec as P

F32, BF16 = jnp.float32, jnp.bfloat16
QB = 256
KC = 256

eps_norm = 1e-06
masked_score = -1e30
highest = lax.Precision.HIGHEST
contract_rows = (((0,), (0,)), ((), ()))
contract_cols = (((1,), (1,)), ((), ()))
contract_table = (((0,), (1,)), ((), ()))


def row_norm(values, gain):
    inverse = lax.rsqrt(jnp.mean(values * values, axis=-1, keepdims=True) + eps_norm)
    return values * inverse * gain


def geglu_mask(gate_values, up_values, keep_column):
    return keep_column * jax.nn.gelu(gate_values, approximate=True) * up_values


def valid_mask(lengths, first_row, row_count, seq_len):
    positions = first_row + lax.iota(jnp.int32, row_count)
    owners = positions // seq_len
    within = positions % seq_len
    chosen = owners[:, None] == lax.iota(jnp.int32, lengths.shape[0])[None, :]
    limits = jnp.sum(jnp.where(chosen, lengths[None, :], 0), axis=1)
    return (within < limits).astype(jnp.float32)


def bucket_rows(buckets, bias_table):
    one_hot = (buckets[:, None] == lax.iota(jnp.int32, bias_table.shape[0])[None, :]).astype(
        jnp.float32
    )
    relative = lax.dot_general(
        bias_table.astype(jnp.float32), one_hot, contract_table, precision=highest
    )
    return (one_hot, relative)


NT = (((1,), (1,)), ((), ()))
TN = (((0,), (0,)), ((), ()))
NN = (((1,), (0,)), ((), ()))

def dot(a, b, dims=NN):
    return lax.dot_general(a, b, dims, preferred_element_type=F32)

def split3(v):
    hi = v.astype(BF16); r = v - hi.astype(F32)
    mid = r.astype(BF16); r = r - mid.astype(F32)
    return hi, mid, r.astype(BF16)

def fill_band(band, row):
    rows, span = band.shape
    base = pltpu.roll(jnp.broadcast_to(row, (8, span)), 0, 1, stride=1, stride_axis=0)
    for g in range(rows // 8):
        band[8 * g:8 * g + 8, :] = pltpu.roll(base, 8 * g, 1) if g else base

def fwd_kernel(len_ref, rel_ref, qkv_ref, mixed_ref, qa_ref, ka_ref, va_ref, band):
    head = pl.program_id(0)
    heads = pl.num_programs(0)
    seq = qkv_ref.shape[0]
    nheads = mixed_ref.shape[1] // 64
    hd = 64
    local = nheads * hd
    length = len_ref[0]
    lane = lax.broadcasted_iota(jnp.int32, (seq, 128), 1)
    row = lax.broadcasted_iota(jnp.int32, (seq, 128), 0)
    for h in range(nheads):
        @pl.when(head == h)
        def _():
            pad = jnp.zeros((seq, 64), BF16)
            q = qkv_ref[:, h * hd:(h + 1) * hd] * jnp.asarray(hd ** -0.5, BF16)
            k = qkv_ref[:, local + h * hd:local + (h + 1) * hd]
            v = qkv_ref[:, 2 * local + h * hd:2 * local + (h + 1) * hd]
            one = jnp.ones((), BF16)
            qa_ref[0] = jnp.where(lane == 67, one, jnp.concatenate([q, pad], axis=1))
            kx = jnp.where((lane >= 64) & (lane < 67), one, jnp.concatenate([k, pad], axis=1))
            ka_ref[0] = jnp.where((lane == 67) & (row >= length), jnp.asarray(-1e30, BF16), kx)
            va_ref[0] = jnp.where((lane >= 64) & (lane < 67), one, jnp.concatenate([v, pad], axis=1))
    fill_band(band, rel_ref[0])
    blane = lax.broadcasted_iota(jnp.int32, (QB, 128), 1)

    def block(step, carry):
        q0 = pl.multiple_of(step * QB, QB)
        q = qa_ref[0, pl.ds(q0, QB), :]
        start = pl.multiple_of(seq - q0, QB)
        s = dot(q, ka_ref[0], NT) + band[:, pl.ds(start, seq)]
        m = jnp.max(s, axis=1, keepdims=True)
        p = jnp.exp(s - m)
        total = jnp.sum(p, axis=1, keepdims=True)
        o = dot(p.astype(BF16), va_ref[0])
        rows = q0 + lax.broadcasted_iota(jnp.int32, (QB, 1), 0)
        keep = (rows < length).astype(F32)
        o = (o[:, :hd] * (keep / total)).astype(BF16)
        for h in range(nheads):
            @pl.when(head == h)
            def _():
                mixed_ref[pl.ds(q0, QB), h * hd:(h + 1) * hd] = o
        lse = -(m + jnp.log(total))
        hi, mid, lo = split3(lse)
        qa_ref[0, pl.ds(q0, QB), :] = jnp.where(blane == 64, hi, jnp.where(blane == 65, mid, jnp.where(blane == 66, lo, q)))
        return carry
    lax.fori_loop(0, seq // QB, block, 0)

def attend(length, rel, qkv, heads):
    seq = qkv.shape[0]
    span = rel.shape[-1]
    aug = jax.ShapeDtypeStruct((heads, seq, 128), BF16)
    aspec = pl.BlockSpec((1, seq, 128), lambda h: (h, 0, 0))
    return pl.pallas_call(
        fwd_kernel, grid=(heads,),
        out_shape=(jax.ShapeDtypeStruct((seq, heads * 64), BF16), aug, aug, aug),
        in_specs=[pl.BlockSpec(memory_space=pltpu.SMEM), pl.BlockSpec((1, 1, span), lambda h: (h, 0, 0)),
                  pl.BlockSpec((seq, 3 * heads * 64), lambda h: (0, 0))],
        out_specs=(pl.BlockSpec((seq, heads * 64), lambda h: (0, 0)), aspec, aspec, aspec),
        scratch_shapes=[pltpu.VMEM((QB, span), F32)],
        compiler_params=pltpu.CompilerParams(vmem_limit_bytes=56 << 20),
        name="attend_fwd",
    )(length, rel.reshape(heads, 1, span), qkv)

def bwd_kernel(rev_ref, dmix_ref, mixed_ref, qa_ref, ka_ref, va_ref, grads_ref, grev_ref, band, gband, da, kt, dq):
    head = pl.program_id(0)
    seq = qa_ref.shape[1]
    hd = 64
    nheads = mixed_ref.shape[1] // hd
    local = nheads * hd
    lane = lax.broadcasted_iota(jnp.int32, (seq, 128), 1)
    for h in range(nheads):
        @pl.when(head == h)
        def _():
            g = dmix_ref[:, h * hd:(h + 1) * hd]
            o = mixed_ref[:, h * hd:(h + 1) * hd]
            inner = -jnp.sum(g.astype(F32) * o.astype(F32), axis=1, keepdims=True)
            hi, mid, lo = split3(inner)
            gx = jnp.concatenate([g, jnp.zeros((seq, 64), BF16)], axis=1)
            da[...] = jnp.where(lane == 64, hi, jnp.where(lane == 65, mid, jnp.where(lane == 66, lo, gx)))
    kt[...] = ka_ref[0].astype(F32).T.astype(BF16)
    fill_band(band, rev_ref[0])
    gband[...] = jnp.zeros_like(gband)
    dq[...] = jnp.zeros_like(dq)

    def block(step, carry):
        k0 = pl.multiple_of(step * QB, QB)
        k = ka_ref[0, pl.ds(k0, QB), :]
        v = va_ref[0, pl.ds(k0, QB), :]
        ktb = kt[:, pl.ds(k0, QB)]
        dv = jnp.zeros((QB, 128), F32)
        dk = jnp.zeros((QB, 128), F32)
        for c in range(seq // KC):
            cols = slice(c * KC, (c + 1) * KC)
            off = pl.ds(pl.multiple_of(seq - k0 + c * KC, KC), KC)
            qc = qa_ref[0, cols, :]
            dc = da[cols, :]
            p = jnp.exp(dot(k, qc, NT) + band[:, off])
            ds = p * dot(v, dc, NT)
            gband[:, off] += ds
            pb = p.astype(BF16)
            db = ds.astype(BF16)
            dv += dot(pb, dc)
            dk += dot(db, qc)
            dq[:, cols] += dot(ktb, db)
        for h in range(nheads):
            @pl.when(head == h)
            def _():
                grads_ref[pl.ds(k0, QB), local + h * hd:local + (h + 1) * hd] = dk[:, :hd].astype(BF16)
                grads_ref[pl.ds(k0, QB), 2 * local + h * hd:2 * local + (h + 1) * hd] = dv[:, :hd].astype(BF16)
        return carry
    lax.fori_loop(0, seq // QB, block, 0)
    for h in range(nheads):
        @pl.when(head == h)
        def _():
            dqt = (dq[...] * (hd ** -0.5)).T
            grads_ref[:, h * hd:(h + 1) * hd] = dqt[:, :hd].astype(BF16)
    span = gband.shape[1]
    acc = gband[0:8, :]
    for g in range(1, QB // 8):
        acc = acc + pltpu.roll(gband[8 * g:8 * g + 8, :], span - 8 * g, 1)
    sub = lax.broadcasted_iota(jnp.int32, (8, span), 0)
    for bit in (1, 2, 4):
        acc = jnp.where((sub & bit) != 0, pltpu.roll(acc, span - bit, 1), acc)
    grev_ref[0] = jnp.sum(acc, axis=0, keepdims=True)

def attend_back(rev, dmix, mixed, qa, ka, va):
    heads, seq, _ = qa.shape
    span = rev.shape[-1]
    aspec = pl.BlockSpec((1, seq, 128), lambda h: (h, 0, 0))
    whole = lambda w: pl.BlockSpec((seq, w), lambda h: (0, 0))
    rspec = pl.BlockSpec((1, 1, span), lambda h: (h, 0, 0))
    grads, grev = pl.pallas_call(
        bwd_kernel, grid=(heads,),
        out_shape=(jax.ShapeDtypeStruct((seq, 3 * heads * 64), BF16), jax.ShapeDtypeStruct((heads, 1, span), F32)),
        in_specs=[rspec, whole(heads * 64), whole(heads * 64), aspec, aspec, aspec],
        out_specs=(whole(3 * heads * 64), rspec),
        scratch_shapes=[pltpu.VMEM((QB, span), F32), pltpu.VMEM((QB, span), F32), pltpu.VMEM((seq, 128), BF16),
                        pltpu.VMEM((128, seq), BF16), pltpu.VMEM((128, seq), F32)],
        compiler_params=pltpu.CompilerParams(vmem_limit_bytes=56 << 20),
        name="attend_bwd",
    )(rev.reshape(heads, 1, span), dmix, mixed, qa, ka, va)
    return grads, grev.reshape(heads, span)


def on_device(
    inputs,
    teacher,
    lengths,
    buckets,
    gain_attn,
    w_query,
    w_key,
    w_value,
    w_out,
    bias_table,
    gain_ff,
    w_gate,
    w_up,
    w_down,
):
    row_count, model_width = inputs.shape
    group_size = lax.axis_size("tensor")
    seq_len = buckets.shape[0] // 2
    all_rows = row_count * group_size
    local_width = w_query.shape[1]
    heads_here = bias_table.shape[1]
    ff_width = w_gate.shape[1]
    my_first = lax.axis_index("tensor") * row_count
    keep_mine = valid_mask(lengths, my_first, row_count, seq_len)
    keep_all = valid_mask(lengths, 0, all_rows, seq_len)
    reversed_buckets = jnp.concatenate([buckets[:1], jnp.flip(buckets[1:])])
    _, relative = bucket_rows(buckets, bias_table)
    one_hot, backward_relative = bucket_rows(reversed_buckets, bias_table)
    gain_a = gain_attn.astype(jnp.float32)
    gain_f = gain_ff.astype(jnp.float32)
    source = inputs.astype(jnp.float32)
    normed = row_norm(source, gain_a).astype(jnp.bfloat16)
    normed_all = lax.all_gather(normed, "tensor", axis=0, tiled=True)
    w_joint = jnp.concatenate([w_query, w_key, w_value], axis=1)

    joint = jnp.dot(normed_all, w_joint, preferred_element_type=jnp.float32).astype(jnp.bfloat16)
    mixed_parts, query_aug, key_aug, value_aug = attend(lengths, relative, joint, heads_here)
    middle = source + lax.psum_scatter(
        jnp.dot(mixed_parts, w_out, preferred_element_type=jnp.float32).astype(jnp.bfloat16),
        "tensor",
        scatter_dimension=0,
        tiled=True,
    ).astype(jnp.float32)
    normed_ff = row_norm(middle, gain_f).astype(jnp.bfloat16)
    normed_ff_all = lax.all_gather(normed_ff, "tensor", axis=0, tiled=True)
    w_pair = jnp.concatenate([w_gate, w_up], axis=1)
    paired = jnp.dot(normed_ff_all, w_pair, preferred_element_type=jnp.float32)
    gate_values = paired[:, :ff_width]
    up_values = paired[:, ff_width:]
    hidden = geglu_mask(gate_values, up_values, keep_all[:, None]).astype(jnp.bfloat16)
    output = middle + lax.psum_scatter(
        jnp.dot(hidden, w_down, preferred_element_type=jnp.float32).astype(jnp.bfloat16),
        "tensor",
        scatter_dimension=0,
        tiled=True,
    ).astype(jnp.float32)
    activations = output.astype(jnp.bfloat16)
    cotangent = keep_mine[:, None] * (output - teacher.astype(jnp.float32))
    loss_part = jnp.sum(cotangent * cotangent)
    count_part = jnp.sum(keep_mine)
    shard_piece = lax.all_gather(cotangent.astype(jnp.bfloat16), "tensor", axis=0, tiled=True)
    grad_down_acc = lax.dot_general(
        hidden, shard_piece, contract_rows, preferred_element_type=jnp.float32
    )
    grad_rows = lax.dot_general(
        shard_piece, w_down, contract_cols, preferred_element_type=jnp.float32
    )
    grad_down = grad_down_acc
    grad_hidden = grad_rows
    _, geglu_back = jax.vjp(
        lambda gate_in, up_in: geglu_mask(gate_in, up_in, keep_all[:, None]), gate_values, up_values
    )
    grad_gate_rows, grad_up_rows = geglu_back(grad_hidden)
    grad_pair = jnp.concatenate([grad_gate_rows, grad_up_rows], axis=1).astype(jnp.bfloat16)
    grad_w_pair = lax.dot_general(
        normed_ff_all, grad_pair, contract_rows, preferred_element_type=jnp.float32
    )
    grad_normed_ff = lax.psum_scatter(
        lax.dot_general(
            grad_pair, w_pair, contract_cols, preferred_element_type=jnp.float32
        ).astype(jnp.bfloat16),
        "tensor",
        scatter_dimension=0,
        tiled=True,
    ).astype(jnp.float32)
    _, norm_back_ff = jax.vjp(row_norm, middle, gain_f)
    grad_middle_part, grad_gain_ff = norm_back_ff(grad_normed_ff)
    grad_middle = cotangent + grad_middle_part
    shard_piece = lax.all_gather(grad_middle.astype(jnp.bfloat16), "tensor", axis=0, tiled=True)
    grad_out_acc = lax.dot_general(
        mixed_parts, shard_piece, contract_rows, preferred_element_type=jnp.float32
    )
    grad_rows = lax.dot_general(
        shard_piece, w_out, contract_cols, preferred_element_type=jnp.float32
    )
    grad_out = grad_out_acc
    grad_mix = grad_rows.astype(jnp.bfloat16) * keep_all[:, None].astype(jnp.bfloat16)
    grad_parts, grad_relative = attend_back(
        backward_relative, grad_mix, mixed_parts, query_aug, key_aug, value_aug
    )
    grad_w_joint = lax.dot_general(
        normed_all, grad_parts, contract_rows, preferred_element_type=jnp.float32
    )
    grad_table = lax.dot_general(one_hot, grad_relative, contract_table, precision=highest)
    grad_normed = lax.psum_scatter(
        lax.dot_general(
            grad_parts, w_joint, contract_cols, preferred_element_type=jnp.float32
        ).astype(jnp.bfloat16),
        "tensor",
        scatter_dimension=0,
        tiled=True,
    ).astype(jnp.float32)
    _, norm_back_attn = jax.vjp(row_norm, source, gain_a)
    grad_source_part, grad_gain_attn = norm_back_attn(grad_normed)
    grad_source = grad_middle + grad_source_part
    gain_attn_total, gain_ff_total, loss_total, count_total = lax.psum(
        (grad_gain_attn, grad_gain_ff, loss_part, count_part), ("dp", "tensor")
    )
    grad_w_joint, grad_out, grad_table, grad_w_pair, grad_down = lax.psum(
        (grad_w_joint, grad_out, grad_table, grad_w_pair, grad_down), "dp"
    )
    factor = 2.0 / (count_total * model_width)
    loss = loss_total / (count_total * model_width)
    return (
        activations,
        loss,
        grad_source * factor,
        gain_attn_total * factor,
        grad_w_joint[:, :local_width] * factor,
        grad_w_joint[:, local_width : 2 * local_width] * factor,
        grad_w_joint[:, 2 * local_width :] * factor,
        grad_out * factor,
        grad_table * factor,
        gain_ff_total * factor,
        grad_w_pair[:, :ff_width] * factor,
        grad_w_pair[:, ff_width:] * factor,
        grad_down * factor,
    )


def solution(mesh):
    in_specs = (
        P(("dp", "tensor"), None),
        P(("dp", "tensor"), None),
        P("dp"),
        P(),
        P(),
        P(None, "tensor"),
        P(None, "tensor"),
        P(None, "tensor"),
        P("tensor", None),
        P(None, "tensor"),
        P(),
        P(None, "tensor"),
        P(None, "tensor"),
        P("tensor", None),
    )
    out_specs = (
        P(("dp", "tensor"), None),
        P(),
        P(("dp", "tensor"), None),
        P(),
        P(None, "tensor"),
        P(None, "tensor"),
        P(None, "tensor"),
        P("tensor", None),
        P(None, "tensor"),
        P(),
        P(None, "tensor"),
        P(None, "tensor"),
        P("tensor", None),
    )
    return jax.shard_map(
        on_device, mesh=mesh, in_specs=in_specs, out_specs=out_specs, check_vma=False
    )
```

```python
import functools

import jax
import jax.numpy as jnp
from jax import lax
from jax.experimental import pallas as pl
from jax.experimental.pallas import tpu as pltpu
from jax.sharding import PartitionSpec as P

F32, BF16 = jnp.float32, jnp.bfloat16
MESH = pl.DeviceIdType.MESH
NT = (((1,), (1,)), ((), ()))
TN = (((0,), (0,)), ((), ()))
NN = (((1,), (0,)), ((), ()))
QB = 256
KC = 256
CHUNKS = 4
eps_norm = 1e-06
highest = lax.Precision.HIGHEST
contract_rows = (((0,), (0,)), ((), ()))
contract_table = (((0,), (1,)), ((), ()))


def dot(a, b, dims=NN):
    return lax.dot_general(a, b, dims, preferred_element_type=F32)


def row_norm(values, gain):
    inverse = lax.rsqrt(jnp.mean(values * values, axis=-1, keepdims=True) + eps_norm)
    return values * inverse * gain


def geglu_mask(gate_values, up_values, keep_column):
    return keep_column * jax.nn.gelu(gate_values, approximate=True) * up_values


def bucket_rows(buckets, bias_table):
    one_hot = (buckets[:, None] == lax.iota(jnp.int32, bias_table.shape[0])[None, :]).astype(F32)
    relative = lax.dot_general(bias_table.astype(F32), one_hot, contract_table, precision=highest)
    return (one_hot, relative)


def split3(v):
    hi = v.astype(BF16); r = v - hi.astype(F32)
    mid = r.astype(BF16); r = r - mid.astype(F32)
    return hi, mid, r.astype(BF16)

def fill_band(band, row):
    rows, span = band.shape
    base = pltpu.roll(jnp.broadcast_to(row, (8, span)), 0, 1, stride=1, stride_axis=0)
    for g in range(rows // 8):
        band[8 * g:8 * g + 8, :] = pltpu.roll(base, 8 * g, 1) if g else base

def fwd_kernel(len_ref, rel_ref, qkv_ref, mixed_ref, qa_ref, ka_ref, va_ref, band):
    head = pl.program_id(0)
    heads = pl.num_programs(0)
    seq = qkv_ref.shape[0]
    nheads = mixed_ref.shape[1] // 64
    hd = 64
    local = nheads * hd
    length = len_ref[0]
    lane = lax.broadcasted_iota(jnp.int32, (seq, 128), 1)
    row = lax.broadcasted_iota(jnp.int32, (seq, 128), 0)
    for h in range(nheads):
        @pl.when(head == h)
        def _():
            pad = jnp.zeros((seq, 64), BF16)
            q = qkv_ref[:, h * hd:(h + 1) * hd] * jnp.asarray(hd ** -0.5, BF16)
            k = qkv_ref[:, local + h * hd:local + (h + 1) * hd]
            v = qkv_ref[:, 2 * local + h * hd:2 * local + (h + 1) * hd]
            one = jnp.ones((), BF16)
            qa_ref[0] = jnp.where(lane == 67, one, jnp.concatenate([q, pad], axis=1))
            kx = jnp.where((lane >= 64) & (lane < 67), one, jnp.concatenate([k, pad], axis=1))
            ka_ref[0] = jnp.where((lane == 67) & (row >= length), jnp.asarray(-1e30, BF16), kx)
            va_ref[0] = jnp.where((lane >= 64) & (lane < 67), one, jnp.concatenate([v, pad], axis=1))
    fill_band(band, rel_ref[0])
    blane = lax.broadcasted_iota(jnp.int32, (QB, 128), 1)

    def block(step, carry):
        q0 = pl.multiple_of(step * QB, QB)
        q = qa_ref[0, pl.ds(q0, QB), :]
        start = pl.multiple_of(seq - q0, QB)
        s = dot(q, ka_ref[0], NT) + band[:, pl.ds(start, seq)]
        m = jnp.max(s, axis=1, keepdims=True)
        p = jnp.exp(s - m)
        total = jnp.sum(p, axis=1, keepdims=True)
        o = dot(p.astype(BF16), va_ref[0])
        rows = q0 + lax.broadcasted_iota(jnp.int32, (QB, 1), 0)
        keep = (rows < length).astype(F32)
        o = (o[:, :hd] * (keep / total)).astype(BF16)
        for h in range(nheads):
            @pl.when(head == h)
            def _():
                mixed_ref[pl.ds(q0, QB), h * hd:(h + 1) * hd] = o
        lse = -(m + jnp.log(total))
        hi, mid, lo = split3(lse)
        qa_ref[0, pl.ds(q0, QB), :] = jnp.where(blane == 64, hi, jnp.where(blane == 65, mid, jnp.where(blane == 66, lo, q)))
        return carry
    lax.fori_loop(0, seq // QB, block, 0)

def attend(length, rel, qkv, heads):
    seq = qkv.shape[0]
    span = rel.shape[-1]
    aug = jax.ShapeDtypeStruct((heads, seq, 128), BF16)
    aspec = pl.BlockSpec((1, seq, 128), lambda h: (h, 0, 0))
    return pl.pallas_call(
        fwd_kernel, grid=(heads,),
        out_shape=(jax.ShapeDtypeStruct((seq, heads * 64), BF16), aug, aug, aug),
        in_specs=[pl.BlockSpec(memory_space=pltpu.SMEM), pl.BlockSpec((1, 1, span), lambda h: (h, 0, 0)),
                  pl.BlockSpec((seq, 3 * heads * 64), lambda h: (0, 0))],
        out_specs=(pl.BlockSpec((seq, heads * 64), lambda h: (0, 0)), aspec, aspec, aspec),
        scratch_shapes=[pltpu.VMEM((QB, span), F32)],
        compiler_params=pltpu.CompilerParams(vmem_limit_bytes=56 << 20),
        name="attend_fwd",
    )(length, rel.reshape(heads, 1, span), qkv)

def bwd_kernel(rev_ref, dmix_ref, mixed_ref, qa_ref, ka_ref, va_ref, grads_ref, grev_ref, band, gband, da, kt, dq):
    head = pl.program_id(0)
    seq = qa_ref.shape[1]
    hd = 64
    nheads = mixed_ref.shape[1] // hd
    local = nheads * hd
    lane = lax.broadcasted_iota(jnp.int32, (seq, 128), 1)
    for h in range(nheads):
        @pl.when(head == h)
        def _():
            g = dmix_ref[:, h * hd:(h + 1) * hd]
            o = mixed_ref[:, h * hd:(h + 1) * hd]
            inner = -jnp.sum(g.astype(F32) * o.astype(F32), axis=1, keepdims=True)
            hi, mid, lo = split3(inner)
            gx = jnp.concatenate([g, jnp.zeros((seq, 64), BF16)], axis=1)
            da[...] = jnp.where(lane == 64, hi, jnp.where(lane == 65, mid, jnp.where(lane == 66, lo, gx)))
    kt[...] = ka_ref[0].astype(F32).T.astype(BF16)
    fill_band(band, rev_ref[0])
    gband[...] = jnp.zeros_like(gband)
    dq[...] = jnp.zeros_like(dq)

    def block(step, carry):
        k0 = pl.multiple_of(step * QB, QB)
        k = ka_ref[0, pl.ds(k0, QB), :]
        v = va_ref[0, pl.ds(k0, QB), :]
        ktb = kt[:, pl.ds(k0, QB)]
        dv = jnp.zeros((QB, 128), F32)
        dk = jnp.zeros((QB, 128), F32)
        for c in range(seq // KC):
            cols = slice(c * KC, (c + 1) * KC)
            off = pl.ds(pl.multiple_of(seq - k0 + c * KC, KC), KC)
            qc = qa_ref[0, cols, :]
            dc = da[cols, :]
            p = jnp.exp(dot(k, qc, NT) + band[:, off])
            ds = p * dot(v, dc, NT)
            gband[:, off] += ds
            pb = p.astype(BF16)
            db = ds.astype(BF16)
            dv += dot(pb, dc)
            dk += dot(db, qc)
            dq[:, cols] += dot(ktb, db)
        for h in range(nheads):
            @pl.when(head == h)
            def _():
                grads_ref[pl.ds(k0, QB), local + h * hd:local + (h + 1) * hd] = dk[:, :hd].astype(BF16)
                grads_ref[pl.ds(k0, QB), 2 * local + h * hd:2 * local + (h + 1) * hd] = dv[:, :hd].astype(BF16)
        return carry
    lax.fori_loop(0, seq // QB, block, 0)
    for h in range(nheads):
        @pl.when(head == h)
        def _():
            dqt = (dq[...] * (hd ** -0.5)).T
            grads_ref[:, h * hd:(h + 1) * hd] = dqt[:, :hd].astype(BF16)
    span = gband.shape[1]
    acc = gband[0:8, :]
    for g in range(1, QB // 8):
        acc = acc + pltpu.roll(gband[8 * g:8 * g + 8, :], span - 8 * g, 1)
    sub = lax.broadcasted_iota(jnp.int32, (8, span), 0)
    for bit in (1, 2, 4):
        acc = jnp.where((sub & bit) != 0, pltpu.roll(acc, span - bit, 1), acc)
    grev_ref[0] = jnp.sum(acc, axis=0, keepdims=True)

def attend_back(rev, dmix, mixed, qa, ka, va):
    heads, seq, _ = qa.shape
    span = rev.shape[-1]
    aspec = pl.BlockSpec((1, seq, 128), lambda h: (h, 0, 0))
    whole = lambda w: pl.BlockSpec((seq, w), lambda h: (0, 0))
    rspec = pl.BlockSpec((1, 1, span), lambda h: (h, 0, 0))
    grads, grev = pl.pallas_call(
        bwd_kernel, grid=(heads,),
        out_shape=(jax.ShapeDtypeStruct((seq, 3 * heads * 64), BF16), jax.ShapeDtypeStruct((heads, 1, span), F32)),
        in_specs=[rspec, whole(heads * 64), whole(heads * 64), aspec, aspec, aspec],
        out_specs=(whole(3 * heads * 64), rspec),
        scratch_shapes=[pltpu.VMEM((QB, span), F32), pltpu.VMEM((QB, span), F32), pltpu.VMEM((seq, 128), BF16),
                        pltpu.VMEM((128, seq), BF16), pltpu.VMEM((128, seq), F32)],
        compiler_params=pltpu.CompilerParams(vmem_limit_bytes=56 << 20),
        name="attend_bwd",
    )(rev.reshape(heads, 1, span), dmix, mixed, qa, ka, va)
    return grads, grev.reshape(heads, span)


def partners():
    me = lax.axis_index("tensor")
    near = me + 1 - 2 * (me % 2)
    far = (me + 2) % 4
    return me, near, far, (near + 2) % 4

def meet(*others):
    barrier = pltpu.get_barrier_semaphore()
    for other in others:
        pl.semaphore_signal(barrier, inc=1, device_id=other, device_id_type=MESH)
    pl.semaphore_wait(barrier, len(others))

def send(src, dst, sems, device):
    return pltpu.make_async_remote_copy(src_ref=src, dst_ref=dst, send_sem=sems.at[0], recv_sem=sems.at[1],
                                        device_id=device, device_id_type=MESH)

def gather_kernel(dims, masked, len_ref, x_ref, w_ref, all_ref, y_ref, land, near_sem, far_sem, pass_sem, out_sem):
    me, near, far, diag = partners()
    rows = x_ref.shape[0]
    size = rows // CHUNKS
    meet({"tensor": near}, {"tensor": far})
    mine = pl.ds(pl.multiple_of(me * rows, rows), rows)
    to_near = send(x_ref, land.at[mine], near_sem, {"tensor": near})
    to_near.start()
    to_far = []
    for c in range(CHUNKS):
        part = pl.ds(pl.multiple_of(me * rows + c * size, size), size)
        copy = send(x_ref.at[pl.ds(c * size, size)], land.at[part], far_sem.at[c], {"tensor": far})
        copy.start()
        to_far.append(copy)
    own = pltpu.make_async_copy(x_ref, all_ref.at[mine], out_sem.at[0])
    own.start()

    def project(part, value):
        y = dot(value, w_ref[...], dims)
        if masked:
            pos = part.start + lax.broadcasted_iota(jnp.int32, y.shape, 0)
            y = jnp.where(pos < len_ref[0], y, 0.0)
        y_ref[part, :] = y.astype(BF16)

    for c in range(CHUNKS):
        project(pl.ds(pl.multiple_of(me * rows + c * size, size), size), x_ref[pl.ds(c * size, size), :])
    to_near.wait_recv()
    for c in range(CHUNKS):
        part = pl.ds(pl.multiple_of(near * rows + c * size, size), size)
        project(part, land[part, :])
    passed = []
    for c in range(CHUNKS):
        to_far[c].wait_recv()
        part = pl.ds(pl.multiple_of(far * rows + c * size, size), size)
        copy = send(land.at[part], land.at[part], pass_sem.at[c], {"tensor": near})
        copy.start()
        passed.append(copy)
        project(part, land[part, :])
    outs = []
    for i, who in enumerate((near, far)):
        part = pl.ds(pl.multiple_of(who * rows, rows), rows)
        copy = pltpu.make_async_copy(land.at[part], all_ref.at[part], out_sem.at[1 + i])
        copy.start()
        outs.append(copy)
    for c in range(CHUNKS):
        passed[c].wait_recv()
        part = pl.ds(pl.multiple_of(diag * rows + c * size, size), size)
        project(part, land[part, :])
    part = pl.ds(pl.multiple_of(diag * rows, rows), rows)
    copy = pltpu.make_async_copy(land.at[part], all_ref.at[part], out_sem.at[3])
    copy.start()
    outs.append(copy)
    to_near.wait_send()
    for copy in to_far + passed:
        copy.wait_send()
    own.wait()
    for copy in outs:
        copy.wait()

def gather_project(x, w, length, dims, masked, collective_id):
    rows, width = x.shape
    out = w.shape[1] if dims is NN else w.shape[0]
    dma = pltpu.SemaphoreType.DMA
    vmem = pl.BlockSpec(memory_space=pltpu.VMEM)
    return pl.pallas_call(
        functools.partial(gather_kernel, dims, masked),
        out_shape=(jax.ShapeDtypeStruct((4 * rows, width), BF16), jax.ShapeDtypeStruct((4 * rows, out), BF16)),
        in_specs=[pl.BlockSpec(memory_space=pltpu.SMEM), vmem, vmem],
        out_specs=(pl.BlockSpec(memory_space=pl.ANY), vmem),
        scratch_shapes=[pltpu.VMEM((4 * rows, width), BF16), dma((2,)), dma((CHUNKS, 2)), dma((CHUNKS, 2)), dma((4,))],
        compiler_params=pltpu.CompilerParams(collective_id=collective_id, has_side_effects=True, vmem_limit_bytes=40 << 20),
        cost_estimate=pl.CostEstimate(flops=8 * rows * width * out, bytes_accessed=50_000_000, transcendentals=0),
        name="gather_project",
    )(length, x, w)

def scatter_kernel(dims, a_ref, w_ref, y_ref, away, kept, out_far, near_land, far_land, near_sem, far_sem):
    me, near, far, diag = partners()
    rows = y_ref.shape[0]
    size = rows // CHUNKS
    meet({"tensor": near}, {"tensor": far})

    def partial(who, c):
        return dot(a_ref[pl.ds(pl.multiple_of(who * rows + c * size, size), size), :], w_ref[...], dims)

    copies = []
    for i, who in enumerate((diag, near)):
        group = []
        for c in range(CHUNKS):
            part = pl.ds(c * size, size)
            away[i, part, :] = partial(who, c).astype(BF16)
            copy = send(away.at[i, part], near_land.at[i, part], near_sem.at[i, c], {"tensor": near})
            copy.start()
            group.append(copy)
        copies.append(group)
        if i == 0:
            to_far = []
            for c in range(CHUNKS):
                part = pl.ds(c * size, size)
                mine = partial(far, c)
                group[c].wait_recv()
                out_far[part, :] = (mine + near_land[0, part, :].astype(F32)).astype(BF16)
                copy = send(out_far.at[part], far_land.at[part], far_sem.at[c], {"tensor": far})
                copy.start()
                to_far.append(copy)
    for c in range(CHUNKS):
        part = pl.ds(c * size, size)
        mine = partial(me, c)
        copies[1][c].wait_recv()
        kept[part, :] = mine + near_land[1, part, :].astype(F32)
    for c in range(CHUNKS):
        part = pl.ds(c * size, size)
        to_far[c].wait_recv()
        y_ref[part, :] = kept[part, :] + far_land[part, :].astype(F32)
    for copy in copies[0] + copies[1] + to_far:
        copy.wait_send()

def project_scatter(a, w, dims, collective_id):
    rows = a.shape[0] // 4
    out = w.shape[1] if dims is NN else w.shape[0]
    dma = pltpu.SemaphoreType.DMA
    vmem = pl.BlockSpec(memory_space=pltpu.VMEM)
    return pl.pallas_call(
        functools.partial(scatter_kernel, dims),
        out_shape=jax.ShapeDtypeStruct((rows, out), F32),
        in_specs=[vmem, vmem],
        out_specs=vmem,
        scratch_shapes=[pltpu.VMEM((2, rows, out), BF16), pltpu.VMEM((rows, out), F32), pltpu.VMEM((rows, out), BF16),
                        pltpu.VMEM((2, rows, out), BF16), pltpu.VMEM((rows, out), BF16), dma((2, CHUNKS, 2)), dma((CHUNKS, 2))],
        compiler_params=pltpu.CompilerParams(collective_id=collective_id, has_side_effects=True, vmem_limit_bytes=40 << 20),
        cost_estimate=pl.CostEstimate(flops=8 * rows * a.shape[1] * out, bytes_accessed=50_000_000, transcendentals=0),
        name="project_scatter",
    )(a, w)


def reduce_kernel(count, pads, *refs):
    n = lax.axis_size("dp")
    outer = n // 2
    gs, small = refs[:count], refs[count]
    outs, small_out = refs[count + 1:2 * count + 1], refs[2 * count + 1]
    rest = refs[2 * count + 2:]
    works, lands, sums, zlands = (rest[i * count:(i + 1) * count] for i in range(4))
    sland, szland, xsem, zsem, gsem, bsem, ssem, szsem = rest[4 * count:]
    d = lax.axis_index("dp")
    side, o = d % 2, d // 2
    pair = {"dp": d + 1 - 2 * side}
    me, near, far, _ = partners()
    others = [{"dp": ((o + j) % outer) * 2 + side} for j in range(1, outer)]
    meet(pair, *others, {"tensor": near}, {"tensor": far})

    def rows(k, which, piece=None):
        half = pads[k] // 2
        if piece is None:
            return pl.ds(pl.multiple_of(which * half, 16), half)
        size = half // outer
        return pl.ds(pl.multiple_of(which * half + piece * size, 16), size)

    started = []

    def go(copy):
        copy.start()
        started.append(copy)
        return copy

    pending = {}

    def stage0(k):
        g = gs[k]
        if pads[k] == g.shape[0]:
            src = g
        else:
            works[k][0:g.shape[0], :] = g[...]
            src = works[k]
        pending[k, 0] = [go(send(src.at[rows(k, 1 - side)], lands[k], xsem.at[k], pair))]
        return src

    srcs = {}

    def stage1(k):
        pending[k, 0][0].wait_recv()
        half = pads[k] // 2
        sums[k][...] = (srcs[k][rows(k, side), :].astype(F32) + lands[k][...].astype(F32)).astype(BF16)
        size = half // outer
        pending[k, 1] = []
        for j in range(1, outer):
            piece = pl.ds(pl.multiple_of(((o + j) % outer) * size, 16), size)
            pending[k, 1].append(go(send(sums[k].at[piece], zlands[k].at[j - 1], zsem.at[k, j - 1], others[j - 1])))

    def stage2(k):
        half = pads[k] // 2
        size = half // outer
        total = sums[k][pl.ds(pl.multiple_of(o * size, 16), size), :].astype(F32)
        for j in range(1, outer):
            pending[k, 1][j - 1].wait_recv()
            total = total + zlands[k][j - 1].astype(F32)
        mine = rows(k, side, o)
        works[k][mine, :] = total.astype(BF16)
        pending[k, 2] = [go(send(works[k].at[mine], works[k].at[mine], gsem.at[k, j - 1], others[j - 1])) for j in range(1, outer)]

    def stage3(k):
        for copy in pending[k, 2]:
            copy.wait_recv()
        mine = rows(k, side)
        pending[k, 3] = [go(send(works[k].at[mine], works[k].at[mine], bsem.at[k], pair))]

    def stage4(k):
        pending[k, 3][0].wait_recv()
        outs[k][...] = works[k][0:outs[k].shape[0], :]

    stages = (stage0, stage1, stage2, stage3, stage4)

    def small0():
        sland[0] = small[...]
        pending["s", 0] = go(send(sland.at[0], sland.at[1], ssem.at[0], pair))

    def small1():
        pending["s", 0].wait_recv()
        szland[o] = sland[0] + sland[1]
        pending["s", 1] = [go(send(szland.at[o], szland.at[o], szsem.at[j - 1], others[j - 1])) for j in range(1, outer)]

    def small2():
        for copy in pending["s", 1]:
            copy.wait_recv()
        total = szland[0]
        for j in range(1, outer):
            total = total + szland[j]
        sland[2] = total
        pending["s", 2] = go(send(sland.at[2], sland.at[3], ssem.at[1], {"tensor": near}))

    def small3():
        pending["s", 2].wait_recv()
        sland[4] = sland[2] + sland[3]
        pending["s", 3] = go(send(sland.at[4], sland.at[5], ssem.at[2], {"tensor": far}))

    def small4():
        pending["s", 3].wait_recv()
        own = lax.broadcasted_iota(jnp.int32, small.shape, 0) >= small.shape[0] - 1
        small_out[...] = jnp.where(own, sland[2], sland[4] + sland[5])

    smalls = (small0, small1, small2, small3, small4)
    for step in range(count + 4):
        if step < 5:
            smalls[step]()
        for k in range(count):
            at = step - k
            if 0 <= at < 5:
                made = stages[at](k)
                if at == 0:
                    srcs[k] = made
    for copy in started:
        copy.wait_send()

def reduce_all(arrays, small, n, collective_id):
    outer = n // 2
    count = len(arrays)
    pads = [-(-a.shape[0] // (16 * n)) * 16 * n for a in arrays]
    dma = pltpu.SemaphoreType.DMA
    vmem = pl.BlockSpec(memory_space=pltpu.VMEM)
    halves = [p // 2 for p in pads]
    return pl.pallas_call(
        functools.partial(reduce_kernel, count, pads),
        out_shape=tuple(jax.ShapeDtypeStruct(a.shape, BF16) for a in arrays) + (jax.ShapeDtypeStruct(small.shape, F32),),
        in_specs=[vmem] * (count + 1),
        out_specs=(vmem,) * (count + 1),
        scratch_shapes=[pltpu.VMEM((p, a.shape[1]), BF16) for p, a in zip(pads, arrays)]
        + [pltpu.VMEM((h, a.shape[1]), BF16) for h, a in zip(halves, arrays)]
        + [pltpu.VMEM((h, a.shape[1]), BF16) for h, a in zip(halves, arrays)]
        + [pltpu.VMEM((outer - 1, h // outer, a.shape[1]), BF16) for h, a in zip(halves, arrays)]
        + [pltpu.VMEM((6,) + small.shape, F32), pltpu.VMEM((outer,) + small.shape, F32),
           dma((count, 2)), dma((count, outer - 1, 2)), dma((count, outer - 1, 2)), dma((count, 2)), dma((3, 2)), dma((outer - 1, 2))],
        compiler_params=pltpu.CompilerParams(collective_id=collective_id, has_side_effects=True, vmem_limit_bytes=50 << 20),
        name="reduce_all",
    )(*arrays, small)


def on_device(
    inputs,
    teacher,
    lengths,
    buckets,
    gain_attn,
    w_query,
    w_key,
    w_value,
    w_out,
    bias_table,
    gain_ff,
    w_gate,
    w_up,
    w_down,
):
    row_count, model_width = inputs.shape
    group_size = lax.axis_size("tensor")
    dp_size = lax.axis_size("dp")
    seq_len = buckets.shape[0] // 2
    local_width = w_query.shape[1]
    heads_here = bias_table.shape[1]
    ff_width = w_gate.shape[1]
    my_first = lax.axis_index("tensor") * row_count
    keep_mine = (my_first + lax.iota(jnp.int32, row_count) < lengths[0]).astype(F32)[:, None]
    reversed_buckets = jnp.concatenate([buckets[:1], jnp.flip(buckets[1:])])
    _, relative = bucket_rows(buckets, bias_table)
    one_hot, backward_relative = bucket_rows(reversed_buckets, bias_table)
    gain_a = gain_attn.astype(F32)
    gain_f = gain_ff.astype(F32)
    source = inputs.astype(F32)
    normed = row_norm(source, gain_a).astype(BF16)
    w_joint = jnp.concatenate([w_query, w_key, w_value], axis=1)
    normed_all, joint = gather_project(normed, w_joint, lengths, NN, False, 1)

    near_pairs = [(i, i ^ 1) for i in range(group_size)]
    far_pairs = [(i, i ^ 2) for i in range(group_size)]
    near_of = lambda value: lax.ppermute(value, "tensor", near_pairs)
    far_of = lambda value: lax.ppermute(value, "tensor", far_pairs)
    w_pair = jnp.concatenate([w_gate, w_up], axis=1)
    pairs = [w_pair, near_of(w_pair), far_of(w_pair)]
    downs = [w_down, near_of(w_down), far_of(w_down)]
    pairs.append(near_of(pairs[2]))
    downs.append(near_of(downs[2]))

    mixed_parts, query_aug, key_aug, value_aug = attend(lengths, relative, joint, heads_here)
    middle = source + project_scatter(mixed_parts, w_out, NN, 2)
    normed_ff = row_norm(middle, gain_f).astype(BF16)
    gates, ups, hiddens = [], [], []
    output = middle
    for pair, down in zip(pairs, downs):
        paired = dot(normed_ff, pair)
        gates.append(paired[:, :ff_width])
        ups.append(paired[:, ff_width:])
        hiddens.append(geglu_mask(gates[-1], ups[-1], keep_mine).astype(BF16))
        output = output + dot(hiddens[-1], down)
    activations = output.astype(BF16)
    cotangent = keep_mine * (output - teacher.astype(F32))
    loss_part = jnp.sum(cotangent * cotangent)
    count_part = jnp.sum(keep_mine)
    grad_ff_rows = cotangent.astype(BF16)
    grad_normed_ff = 0.0
    down_grads, pair_grads = [], []
    for pair, down, gate, up, hidden in zip(pairs, downs, gates, ups, hiddens):
        grad_hidden = dot(grad_ff_rows, down, NT)
        _, geglu_back = jax.vjp(lambda g, u: geglu_mask(g, u, keep_mine), gate, up)
        grad_pair = jnp.concatenate(geglu_back(grad_hidden), axis=1).astype(BF16)
        grad_normed_ff = grad_normed_ff + dot(grad_pair, pair, NT)
        down_grads.append(dot(hidden, grad_ff_rows, TN))
        pair_grads.append(dot(normed_ff, grad_pair, TN))
    _, norm_back_ff = jax.vjp(row_norm, middle, gain_f)
    grad_middle_part, grad_gain_ff = norm_back_ff(grad_normed_ff)
    grad_middle = cotangent + grad_middle_part

    def share(parts):
        mine, near, far, diag = parts
        total_far = (far + near_of(diag.astype(BF16)).astype(F32)).astype(BF16)
        return (mine + near_of(near.astype(BF16)).astype(F32) + far_of(total_far).astype(F32)).astype(BF16)

    grad_down = share(down_grads)
    grad_pair_sum = share(pair_grads)
    grad_all, grad_mix = gather_project(grad_middle.astype(BF16), w_out, lengths, NT, True, 3)
    grad_out = dot(mixed_parts, grad_all, TN).astype(BF16)
    grad_parts, grad_relative = attend_back(
        backward_relative, grad_mix, mixed_parts, query_aug, key_aug, value_aug
    )
    grad_w_joint = dot(normed_all, grad_parts, TN).astype(BF16)
    grad_table = lax.dot_general(one_hot, grad_relative, contract_table, precision=highest)
    grad_normed = project_scatter(grad_parts, w_joint, NT, 4)
    _, norm_back_attn = jax.vjp(row_norm, source, gain_a)
    grad_source_part, grad_gain_attn = norm_back_attn(grad_normed)
    grad_source = grad_middle + grad_source_part

    gain_rows = model_width // 128
    scalars = jnp.zeros((8, 128), F32).at[0, 0].set(loss_part).at[0, 1].set(count_part)
    table_row = jnp.zeros((8, 128), F32).at[7, : grad_table.size].set(grad_table.reshape(-1))
    small = jnp.concatenate(
        [grad_gain_attn.reshape(gain_rows, 128), grad_gain_ff.reshape(gain_rows, 128), scalars, table_row]
    )
    small = jnp.pad(small, ((small.shape[0] % 8, 0), (0, 0)))
    first = small.shape[0] - 16 - 2 * gain_rows
    rows_here = grad_out.shape[0]
    tall = jnp.concatenate([grad_out, grad_down])
    tall = jnp.pad(tall, ((0, -tall.shape[0] % (16 * dp_size)), (0, 0)))
    grad_gate, grad_up, tall, grad_w_joint, small = reduce_all(
        [grad_pair_sum[:, :ff_width], grad_pair_sum[:, ff_width:], tall, grad_w_joint], small, dp_size, 5
    )
    small = small[first:]
    loss_total, count_total = small[2 * gain_rows, 0], small[2 * gain_rows, 1]
    grad_table = small[-1, : grad_table.size].reshape(grad_table.shape)
    factor = 2.0 / (count_total * model_width)
    scaled = lambda value: value.astype(F32) * factor
    return (
        activations,
        loss_total / (count_total * model_width),
        grad_source * factor,
        small[:gain_rows].reshape(-1) * factor,
        scaled(grad_w_joint[:, :local_width]),
        scaled(grad_w_joint[:, local_width : 2 * local_width]),
        scaled(grad_w_joint[:, 2 * local_width :]),
        scaled(tall[:rows_here]),
        grad_table * factor,
        small[gain_rows : 2 * gain_rows].reshape(-1) * factor,
        scaled(grad_gate),
        scaled(grad_up),
        scaled(tall[rows_here : rows_here + ff_width]),
    )


def solution(mesh):
    in_specs = (
        P(("dp", "tensor"), None),
        P(("dp", "tensor"), None),
        P("dp"),
        P(),
        P(),
        P(None, "tensor"),
        P(None, "tensor"),
        P(None, "tensor"),
        P("tensor", None),
        P(None, "tensor"),
        P(),
        P(None, "tensor"),
        P(None, "tensor"),
        P("tensor", None),
    )
    out_specs = (
        P(("dp", "tensor"), None),
        P(),
        P(("dp", "tensor"), None),
        P(),
        P(None, "tensor"),
        P(None, "tensor"),
        P(None, "tensor"),
        P("tensor", None),
        P(None, "tensor"),
        P(),
        P(None, "tensor"),
        P(None, "tensor"),
        P("tensor", None),
    )
    return jax.shard_map(
        on_device, mesh=mesh, in_specs=in_specs, out_specs=out_specs, check_vma=False
    )
```

```python
import functools

import jax
import jax.numpy as jnp
from jax import lax
from jax.experimental import pallas as pl
from jax.experimental.pallas import tpu as pltpu
from jax.sharding import PartitionSpec as P

F32, BF16 = jnp.float32, jnp.bfloat16
MESH = pl.DeviceIdType.MESH
NT = (((1,), (1,)), ((), ()))
TN = (((0,), (0,)), ((), ()))
NN = (((1,), (0,)), ((), ()))
QB = 256
KC = 256
CHUNKS = 4
eps_norm = 1e-06
highest = lax.Precision.HIGHEST
contract_rows = (((0,), (0,)), ((), ()))
contract_table = (((0,), (1,)), ((), ()))


def dot(a, b, dims=NN):
    return lax.dot_general(a, b, dims, preferred_element_type=F32)


def row_norm(values, gain):
    inverse = lax.rsqrt(jnp.mean(values * values, axis=-1, keepdims=True) + eps_norm)
    return values * inverse * gain


def geglu_mask(gate_values, up_values, keep_column):
    return keep_column * jax.nn.gelu(gate_values, approximate=True) * up_values


def bucket_rows(buckets, bias_table):
    one_hot = (buckets[:, None] == lax.iota(jnp.int32, bias_table.shape[0])[None, :]).astype(F32)
    relative = lax.dot_general(bias_table.astype(F32), one_hot, contract_table, precision=highest)
    return (one_hot, relative)


def split3(v):
    hi = v.astype(BF16); r = v - hi.astype(F32)
    mid = r.astype(BF16); r = r - mid.astype(F32)
    return hi, mid, r.astype(BF16)

def fill_band(band, row):
    rows, span = band.shape
    base = pltpu.roll(jnp.broadcast_to(row, (8, span)), 0, 1, stride=1, stride_axis=0)
    for g in range(rows // 8):
        band[8 * g:8 * g + 8, :] = pltpu.roll(base, 8 * g, 1) if g else base

def fwd_kernel(len_ref, rel_ref, qkv_ref, mixed_ref, qa_ref, ka_ref, va_ref, band):
    head = pl.program_id(0)
    heads = pl.num_programs(0)
    seq = qkv_ref.shape[0]
    nheads = mixed_ref.shape[1] // 64
    hd = 64
    length = len_ref[0]
    lane = lax.broadcasted_iota(jnp.int32, (seq, 128), 1)
    row = lax.broadcasted_iota(jnp.int32, (seq, 128), 0)
    for h in range(nheads):
        @pl.when(head == h)
        def _():
            pad = jnp.zeros((seq, 64), BF16)
            base = 3 * h * hd
            q = qkv_ref[:, base:base + hd] * jnp.asarray(hd ** -0.5, BF16)
            k = qkv_ref[:, base + hd:base + 2 * hd]
            v = qkv_ref[:, base + 2 * hd:base + 3 * hd]
            one = jnp.ones((), BF16)
            qa_ref[0] = jnp.where(lane == 67, one, jnp.concatenate([q, pad], axis=1))
            kx = jnp.where((lane >= 64) & (lane < 67), one, jnp.concatenate([k, pad], axis=1))
            ka_ref[0] = jnp.where((lane == 67) & (row >= length), jnp.asarray(-1e30, BF16), kx)
            va_ref[0] = jnp.where((lane >= 64) & (lane < 67), one, jnp.concatenate([v, pad], axis=1))
    fill_band(band, rel_ref[0])
    blane = lax.broadcasted_iota(jnp.int32, (QB, 128), 1)

    def block(step, carry):
        q0 = pl.multiple_of(step * QB, QB)
        q = qa_ref[0, pl.ds(q0, QB), :]
        start = pl.multiple_of(seq - q0, QB)
        s = dot(q, ka_ref[0], NT) + band[:, pl.ds(start, seq)]
        m = jnp.max(s, axis=1, keepdims=True)
        p = jnp.exp(s - m)
        total = jnp.sum(p, axis=1, keepdims=True)
        o = dot(p.astype(BF16), va_ref[0])
        rows = q0 + lax.broadcasted_iota(jnp.int32, (QB, 1), 0)
        keep = (rows < length).astype(F32)
        o = (o[:, :hd] * (keep / total)).astype(BF16)
        for h in range(nheads):
            @pl.when(head == h)
            def _():
                mixed_ref[pl.ds(q0, QB), h * hd:(h + 1) * hd] = o
        lse = -(m + jnp.log(total))
        hi, mid, lo = split3(lse)
        qa_ref[0, pl.ds(q0, QB), :] = jnp.where(blane == 64, hi, jnp.where(blane == 65, mid, jnp.where(blane == 66, lo, q)))
        return carry
    lax.fori_loop(0, seq // QB, block, 0)

def attend(length, rel, qkv, heads):
    seq = qkv.shape[0]
    span = rel.shape[-1]
    aug = jax.ShapeDtypeStruct((heads, seq, 128), BF16)
    aspec = pl.BlockSpec((1, seq, 128), lambda h: (h, 0, 0))
    return pl.pallas_call(
        fwd_kernel, grid=(heads,),
        out_shape=(jax.ShapeDtypeStruct((seq, heads * 64), BF16), aug, aug, aug),
        in_specs=[pl.BlockSpec(memory_space=pltpu.SMEM), pl.BlockSpec((1, 1, span), lambda h: (h, 0, 0)),
                  pl.BlockSpec((seq, 3 * heads * 64), lambda h: (0, 0))],
        out_specs=(pl.BlockSpec((seq, heads * 64), lambda h: (0, 0)), aspec, aspec, aspec),
        scratch_shapes=[pltpu.VMEM((QB, span), F32)],
        compiler_params=pltpu.CompilerParams(vmem_limit_bytes=56 << 20),
        name="attend_fwd",
    )(length, rel.reshape(heads, 1, span), qkv)

def partners():
    me = lax.axis_index("tensor")
    near = me + 1 - 2 * (me % 2)
    far = (me + 2) % 4
    return me, near, far, (near + 2) % 4

def meet(*others):
    barrier = pltpu.get_barrier_semaphore()
    for other in others:
        pl.semaphore_signal(barrier, inc=1, device_id=other, device_id_type=MESH)
    pl.semaphore_wait(barrier, len(others))

def send(src, dst, sems, device):
    return pltpu.make_async_remote_copy(src_ref=src, dst_ref=dst, send_sem=sems.at[0], recv_sem=sems.at[1],
                                        device_id=device, device_id_type=MESH)

def gather_kernel(dims, masked, len_ref, x_ref, w_ref, all_ref, y_ref, land, near_sem, far_sem, pass_sem, out_sem):
    me, near, far, diag = partners()
    rows = x_ref.shape[0]
    size = rows // CHUNKS
    meet({"tensor": near}, {"tensor": far})
    mine = pl.ds(pl.multiple_of(me * rows, rows), rows)
    to_near = send(x_ref, land.at[mine], near_sem, {"tensor": near})
    to_near.start()
    to_far = []
    for c in range(CHUNKS):
        part = pl.ds(pl.multiple_of(me * rows + c * size, size), size)
        copy = send(x_ref.at[pl.ds(c * size, size)], land.at[part], far_sem.at[c], {"tensor": far})
        copy.start()
        to_far.append(copy)
    own = pltpu.make_async_copy(x_ref, all_ref.at[mine], out_sem.at[0])
    own.start()

    def project(part, value):
        y = dot(value, w_ref[...], dims)
        if masked:
            pos = part.start + lax.broadcasted_iota(jnp.int32, y.shape, 0)
            y = jnp.where(pos < len_ref[0], y, 0.0)
        y_ref[part, :] = y.astype(BF16)

    for c in range(CHUNKS):
        project(pl.ds(pl.multiple_of(me * rows + c * size, size), size), x_ref[pl.ds(c * size, size), :])
    to_near.wait_recv()
    for c in range(CHUNKS):
        part = pl.ds(pl.multiple_of(near * rows + c * size, size), size)
        project(part, land[part, :])
    passed = []
    for c in range(CHUNKS):
        to_far[c].wait_recv()
        part = pl.ds(pl.multiple_of(far * rows + c * size, size), size)
        copy = send(land.at[part], land.at[part], pass_sem.at[c], {"tensor": near})
        copy.start()
        passed.append(copy)
        project(part, land[part, :])
    outs = []
    for i, who in enumerate((near, far)):
        part = pl.ds(pl.multiple_of(who * rows, rows), rows)
        copy = pltpu.make_async_copy(land.at[part], all_ref.at[part], out_sem.at[1 + i])
        copy.start()
        outs.append(copy)
    for c in range(CHUNKS):
        passed[c].wait_recv()
        part = pl.ds(pl.multiple_of(diag * rows + c * size, size), size)
        project(part, land[part, :])
    part = pl.ds(pl.multiple_of(diag * rows, rows), rows)
    copy = pltpu.make_async_copy(land.at[part], all_ref.at[part], out_sem.at[3])
    copy.start()
    outs.append(copy)
    to_near.wait_send()
    for copy in to_far + passed:
        copy.wait_send()
    own.wait()
    for copy in outs:
        copy.wait()

def gather_project(x, w, length, dims, masked, collective_id):
    rows, width = x.shape
    out = w.shape[1] if dims is NN else w.shape[0]
    dma = pltpu.SemaphoreType.DMA
    vmem = pl.BlockSpec(memory_space=pltpu.VMEM)
    return pl.pallas_call(
        functools.partial(gather_kernel, dims, masked),
        out_shape=(jax.ShapeDtypeStruct((4 * rows, width), BF16), jax.ShapeDtypeStruct((4 * rows, out), BF16)),
        in_specs=[pl.BlockSpec(memory_space=pltpu.SMEM), vmem, vmem],
        out_specs=(pl.BlockSpec(memory_space=pl.ANY), vmem),
        scratch_shapes=[pltpu.VMEM((4 * rows, width), BF16), dma((2,)), dma((CHUNKS, 2)), dma((CHUNKS, 2)), dma((4,))],
        compiler_params=pltpu.CompilerParams(collective_id=collective_id, has_side_effects=True, vmem_limit_bytes=40 << 20),
        cost_estimate=pl.CostEstimate(flops=8 * rows * width * out, bytes_accessed=50_000_000, transcendentals=0),
        name="gather_project",
    )(length, x, w)

def scatter_kernel(dims, a_ref, w_ref, y_ref, away, kept, out_far, near_land, far_land, near_sem, far_sem):
    me, near, far, diag = partners()
    rows = y_ref.shape[0]
    size = rows // CHUNKS
    meet({"tensor": near}, {"tensor": far})

    def partial(who, c):
        return dot(a_ref[pl.ds(pl.multiple_of(who * rows + c * size, size), size), :], w_ref[...], dims)

    copies = []
    for i, who in enumerate((diag, near)):
        group = []
        for c in range(CHUNKS):
            part = pl.ds(c * size, size)
            away[i, part, :] = partial(who, c).astype(BF16)
            copy = send(away.at[i, part], near_land.at[i, part], near_sem.at[i, c], {"tensor": near})
            copy.start()
            group.append(copy)
        copies.append(group)
        if i == 0:
            to_far = []
            for c in range(CHUNKS):
                part = pl.ds(c * size, size)
                mine = partial(far, c)
                group[c].wait_recv()
                out_far[part, :] = (mine + near_land[0, part, :].astype(F32)).astype(BF16)
                copy = send(out_far.at[part], far_land.at[part], far_sem.at[c], {"tensor": far})
                copy.start()
                to_far.append(copy)
    for c in range(CHUNKS):
        part = pl.ds(c * size, size)
        mine = partial(me, c)
        copies[1][c].wait_recv()
        kept[part, :] = mine + near_land[1, part, :].astype(F32)
    for c in range(CHUNKS):
        part = pl.ds(c * size, size)
        to_far[c].wait_recv()
        y_ref[part, :] = kept[part, :] + far_land[part, :].astype(F32)
    for copy in copies[0] + copies[1] + to_far:
        copy.wait_send()

def project_scatter(a, w, dims, collective_id):
    rows = a.shape[0] // 4
    out = w.shape[1] if dims is NN else w.shape[0]
    dma = pltpu.SemaphoreType.DMA
    vmem = pl.BlockSpec(memory_space=pltpu.VMEM)
    return pl.pallas_call(
        functools.partial(scatter_kernel, dims),
        out_shape=jax.ShapeDtypeStruct((rows, out), F32),
        in_specs=[vmem, vmem],
        out_specs=vmem,
        scratch_shapes=[pltpu.VMEM((2, rows, out), BF16), pltpu.VMEM((rows, out), F32), pltpu.VMEM((rows, out), BF16),
                        pltpu.VMEM((2, rows, out), BF16), pltpu.VMEM((rows, out), BF16), dma((2, CHUNKS, 2)), dma((CHUNKS, 2))],
        compiler_params=pltpu.CompilerParams(collective_id=collective_id, has_side_effects=True, vmem_limit_bytes=40 << 20),
        cost_estimate=pl.CostEstimate(flops=8 * rows * a.shape[1] * out, bytes_accessed=50_000_000, transcendentals=0),
        name="project_scatter",
    )(a, w)


def reduce_kernel(count, pads, *refs):
    n = lax.axis_size("dp")
    outer = n // 2
    gs, small = refs[:count], refs[count]
    outs, small_out = refs[count + 1:2 * count + 1], refs[2 * count + 1]
    rest = refs[2 * count + 2:]
    works, lands, sums, zlands = (rest[i * count:(i + 1) * count] for i in range(4))
    sland, szland, xsem, zsem, gsem, bsem, ssem, szsem = rest[4 * count:]
    d = lax.axis_index("dp")
    side, o = d % 2, d // 2
    pair = {"dp": d + 1 - 2 * side}
    me, near, far, _ = partners()
    others = [{"dp": ((o + j) % outer) * 2 + side} for j in range(1, outer)]
    meet(pair, *others, {"tensor": near}, {"tensor": far})

    def rows(k, which, piece=None):
        half = pads[k] // 2
        if piece is None:
            return pl.ds(pl.multiple_of(which * half, 16), half)
        size = half // outer
        return pl.ds(pl.multiple_of(which * half + piece * size, 16), size)

    started = []

    def go(copy):
        copy.start()
        started.append(copy)
        return copy

    pending = {}

    def stage0(k):
        g = gs[k]
        if pads[k] == g.shape[0]:
            src = g
        else:
            works[k][0:g.shape[0], :] = g[...]
            src = works[k]
        pending[k, 0] = [go(send(src.at[rows(k, 1 - side)], lands[k], xsem.at[k], pair))]
        return src

    srcs = {}

    def stage1(k):
        pending[k, 0][0].wait_recv()
        half = pads[k] // 2
        sums[k][...] = (srcs[k][rows(k, side), :].astype(F32) + lands[k][...].astype(F32)).astype(BF16)
        size = half // outer
        pending[k, 1] = []
        for j in range(1, outer):
            piece = pl.ds(pl.multiple_of(((o + j) % outer) * size, 16), size)
            pending[k, 1].append(go(send(sums[k].at[piece], zlands[k].at[j - 1], zsem.at[k, j - 1], others[j - 1])))

    def stage2(k):
        half = pads[k] // 2
        size = half // outer
        total = sums[k][pl.ds(pl.multiple_of(o * size, 16), size), :].astype(F32)
        for j in range(1, outer):
            pending[k, 1][j - 1].wait_recv()
            total = total + zlands[k][j - 1].astype(F32)
        mine = rows(k, side, o)
        works[k][mine, :] = total.astype(BF16)
        pending[k, 2] = [go(send(works[k].at[mine], works[k].at[mine], gsem.at[k, j - 1], others[j - 1])) for j in range(1, outer)]

    def stage3(k):
        for copy in pending[k, 2]:
            copy.wait_recv()
        mine = rows(k, side)
        pending[k, 3] = [go(send(works[k].at[mine], works[k].at[mine], bsem.at[k], pair))]

    def stage4(k):
        pending[k, 3][0].wait_recv()
        outs[k][...] = works[k][0:outs[k].shape[0], :]

    stages = (stage0, stage1, stage2, stage3, stage4)

    def small0():
        sland[0] = small[...]
        pending["s", 0] = go(send(sland.at[0], sland.at[1], ssem.at[0], pair))

    def small1():
        pending["s", 0].wait_recv()
        szland[o] = sland[0] + sland[1]
        pending["s", 1] = [go(send(szland.at[o], szland.at[o], szsem.at[j - 1], others[j - 1])) for j in range(1, outer)]

    def small2():
        for copy in pending["s", 1]:
            copy.wait_recv()
        total = szland[0]
        for j in range(1, outer):
            total = total + szland[j]
        sland[2] = total
        pending["s", 2] = go(send(sland.at[2], sland.at[3], ssem.at[1], {"tensor": near}))

    def small3():
        pending["s", 2].wait_recv()
        sland[4] = sland[2] + sland[3]
        pending["s", 3] = go(send(sland.at[4], sland.at[5], ssem.at[2], {"tensor": far}))

    def small4():
        pending["s", 3].wait_recv()
        own = lax.broadcasted_iota(jnp.int32, small.shape, 0) >= small.shape[0] - 1
        small_out[...] = jnp.where(own, sland[2], sland[4] + sland[5])

    smalls = (small0, small1, small2, small3, small4)
    for step in range(max(count, 1) + 4):
        if step < 5:
            smalls[step]()
        for k in range(count):
            at = step - k
            if 0 <= at < 5:
                made = stages[at](k)
                if at == 0:
                    srcs[k] = made
    for copy in started:
        copy.wait_send()

def reduce_all(arrays, small, n, collective_id):
    outer = n // 2
    count = len(arrays)
    pads = [-(-a.shape[0] // (16 * n)) * 16 * n for a in arrays]
    dma = pltpu.SemaphoreType.DMA
    vmem = pl.BlockSpec(memory_space=pltpu.VMEM)
    halves = [p // 2 for p in pads]
    return pl.pallas_call(
        functools.partial(reduce_kernel, count, pads),
        out_shape=tuple(jax.ShapeDtypeStruct(a.shape, BF16) for a in arrays) + (jax.ShapeDtypeStruct(small.shape, F32),),
        in_specs=[vmem] * (count + 1),
        out_specs=(vmem,) * (count + 1),
        scratch_shapes=[pltpu.VMEM((p, a.shape[1]), BF16) for p, a in zip(pads, arrays)]
        + [pltpu.VMEM((h, a.shape[1]), BF16) for h, a in zip(halves, arrays)]
        + [pltpu.VMEM((h, a.shape[1]), BF16) for h, a in zip(halves, arrays)]
        + [pltpu.VMEM((outer - 1, h // outer, a.shape[1]), BF16) for h, a in zip(halves, arrays)]
        + [pltpu.VMEM((6,) + small.shape, F32), pltpu.VMEM((outer,) + small.shape, F32),
           dma((count + 1, 2)), dma((count + 1, outer - 1, 2)), dma((count + 1, outer - 1, 2)), dma((count + 1, 2)), dma((3, 2)), dma((outer - 1, 2))],
        compiler_params=pltpu.CompilerParams(collective_id=collective_id, has_side_effects=True, vmem_limit_bytes=50 << 20),
        name="reduce_all",
    )(*arrays, small)


def sweep(total, body):
    size = total // 8

    def step(i, carry):
        body(pl.ds(pl.multiple_of(i * size, 16), size))
        return carry

    lax.fori_loop(0, 8, step, 0)


def backward_kernel(
    counts, len_ref, gm_ref, w_out_ref, rev_ref, mixed_ref, qa_ref, ka_ref, va_ref, nt_ref, w3_ref, *refs
):
    heads, rows_pad, ff = counts
    parts = (refs[0:4], refs[4:8], refs[8:12])
    downs = parts[2]
    y_ref, grev_ref = refs[12:14]
    outs = refs[14:17 + heads]
    refs = refs[17 + heads:]
    count = 3 + heads
    land, dmix, band, gband, da, kt, dq, grads = refs[:8]
    farp, nland, fland = (refs[8 + 3 * i:11 + 3 * i] for i in range(3))
    refs = refs[17:]
    works, dlands, dsums, zlands = (refs[count * i:count * (i + 1)] for i in range(4))
    refs = refs[4 * count:]
    away, out_far, near_land, far_land = refs[:4]
    (gnear, gfar, gpass, lsem, tnear, tfar, xsem, zsem, gsem, bsem, osem, rnear, rfar) = refs[4:]
    n = lax.axis_size("dp")
    outer = n // 2
    d = lax.axis_index("dp")
    side, o = d % 2, d // 2
    pair = {"dp": d + 1 - 2 * side}
    me, near, far, diag = partners()
    others = [{"dp": ((o + j) % outer) * 2 + side} for j in range(1, outer)]
    rows, width = gm_ref.shape
    seq = qa_ref.shape[1]
    hd = dmix.shape[1] // heads
    meet(pair, *others, {"tensor": near}, {"tensor": far})

    size = rows // CHUNKS
    mine = pl.ds(pl.multiple_of(me * rows, rows), rows)
    spot = lambda who, c: pl.ds(pl.multiple_of(who * rows + c * size, size), size)
    to_near = send(gm_ref, land.at[mine], gnear, {"tensor": near})
    to_near.start()
    to_far = [send(gm_ref.at[pl.ds(c * size, size)], land.at[spot(me, c)], gfar.at[c], {"tensor": far}) for c in range(CHUNKS)]
    for copy in to_far:
        copy.start()
    locals_ = []
    for k in range(3):
        src = parts[k]
        locals_.append(pltpu.make_async_copy(src[0], works[k].at[pl.ds(0, src[0].shape[0])], lsem.at[k, 0]))
        locals_.append(pltpu.make_async_copy(src[2], farp[k], lsem.at[k, 1]))
        for copy in locals_[-2:]:
            copy.start()

    def first(k, i):
        return send(parts[k][(3, 1)[i]], nland[k].at[i], tnear.at[k, i], {"tensor": near})

    for k in range(3):
        for i in range(2):
            first(k, i).start()
    land[mine, :] = gm_ref[...]

    def project(part, value):
        y = dot(value, w_out_ref[...], NT)
        pos = part.start + lax.broadcasted_iota(jnp.int32, y.shape, 0)
        dmix[part, :] = jnp.where(pos < len_ref[0], y, 0.0).astype(BF16)

    for c in range(CHUNKS):
        project(spot(me, c), gm_ref[pl.ds(c * size, size), :])
    to_near.wait_recv()
    for c in range(CHUNKS):
        project(spot(near, c), land[spot(near, c), :])
    passed = []
    for c in range(CHUNKS):
        to_far[c].wait_recv()
        part = spot(far, c)
        copy = send(land.at[part], land.at[part], gpass.at[c], {"tensor": near})
        copy.start()
        passed.append(copy)
        project(part, land[part, :])
    for copy in locals_:
        copy.wait()

    def second(k):
        return send(farp[k], fland[k], tfar.at[k], {"tensor": far})

    def stage_t1(k):
        first(k, 0).wait_recv()

        def add(r):
            farp[k][r, :] = (farp[k][r, :].astype(F32) + nland[k][0, r, :].astype(F32)).astype(BF16)

        sweep(farp[k].shape[0], add)
        second(k).start()

    def half_of(which):
        return pl.ds(pl.multiple_of(which * (rows_pad // 2), 16), rows_pad // 2)

    small_rows = rows_pad // n
    piece_of = lambda at: pl.ds(pl.multiple_of(at * small_rows, 16), small_rows)
    final_of = lambda at: pl.ds(pl.multiple_of(side * (rows_pad // 2) + at * small_rows, 16), small_rows)

    def cross(k):
        return send(dsums[k], dlands[k], xsem.at[k], pair)

    def spread(k, j):
        return send(dsums[k].at[piece_of((o + j) % outer)], zlands[k].at[j - 1], zsem.at[k, j - 1], others[j - 1])

    def collect(k, j):
        return send(works[k].at[final_of(o)], works[k].at[final_of(o)], gsem.at[k, j - 1], others[j - 1])

    def back(k):
        return send(works[k].at[half_of(side)], works[k].at[half_of(side)], bsem.at[k], pair)

    def emit(k):
        return pltpu.make_async_copy(works[k].at[pl.ds(0, outs[k].shape[0])], outs[k], osem.at[k])

    def leave(k):
        dsums[k][...] = works[k][half_of(1 - side), :]
        cross(k).start()

    def stage_t2(k):
        first(k, 1).wait_recv()
        second(k).wait_recv()

        def add(r):
            total = works[k][r, :].astype(F32) + nland[k][1, r, :].astype(F32) + fland[k][r, :].astype(F32)
            works[k][r, :] = total.astype(BF16)

        sweep(farp[k].shape[0], add)
        leave(k)

    def stage_d1(k):
        cross(k).wait_send()
        cross(k).wait_recv()

        def add(r):
            mine = pl.ds(pl.multiple_of(side * (rows_pad // 2) + r.start, 16), r.size)
            dsums[k][r, :] = (works[k][mine, :].astype(F32) + dlands[k][r, :].astype(F32)).astype(BF16)

        sweep(rows_pad // 2, add)
        for j in range(1, outer):
            spread(k, j).start()

    def stage_d2(k):
        total = dsums[k][piece_of(o), :].astype(F32)
        for j in range(1, outer):
            spread(k, j).wait_recv()
            total = total + zlands[k][j - 1].astype(F32)
        works[k][final_of(o), :] = total.astype(BF16)
        for j in range(1, outer):
            collect(k, j).start()

    def stage_d3(k):
        for j in range(1, outer):
            collect(k, j).wait_recv()
        back(k).start()

    def stage_d4(k):
        back(k).wait_recv()
        emit(k).start()

    if rows_pad > width:
        for k in range(count):
            works[k][width:, :] = jnp.zeros_like(works[k][width:, :])
    stage_t1(0)
    for c in range(CHUNKS):
        passed[c].wait_recv()
        project(spot(diag, c), land[spot(diag, c), :])
    tail = rows_pad - downs[0].shape[0]
    out_rows = w_out_ref.shape[0]
    base = downs[0].shape[0]
    works[2][base:base + out_rows, :] = dot(mixed_ref[...], land[...], TN).astype(BF16)
    if tail > out_rows:
        works[2][base + out_rows:, :] = jnp.zeros_like(works[2][base + out_rows:, :])

    events = {
        3: [(stage_t1, 1)], 6: [(stage_t2, 0)], 9: [(stage_t1, 2)], 10: [(stage_d1, 0), (stage_d1, 3)],
        12: [(stage_t2, 1), (stage_d2, 3)], 13: [(stage_d2, 0)], 15: [(stage_d3, 3)], 16: [(stage_d1, 1), (stage_d3, 0)],
        17: [(stage_d4, 3)], 18: [(stage_d1, 4)], 19: [(stage_t2, 2), (stage_d4, 0)], 20: [(stage_d2, 1), (stage_d2, 4)],
        22: [(stage_d3, 4)], 23: [(stage_d1, 2), (stage_d3, 1)],
    }
    lane = lax.broadcasted_iota(jnp.int32, (seq, 128), 1)
    span = gband.shape[1]
    blocks = seq // QB

    def head_body(head, carry):
        for h in range(heads):
            @pl.when(head == h)
            def _():
                g = dmix[:, h * hd:(h + 1) * hd]
                inner = -jnp.sum(g.astype(F32) * mixed_ref[:, h * hd:(h + 1) * hd].astype(F32), axis=1, keepdims=True)
                hi, mid, lo = split3(inner)
                gx = jnp.concatenate([g, jnp.zeros((seq, 128 - hd), BF16)], axis=1)
                da[...] = jnp.where(lane == hd, hi, jnp.where(lane == hd + 1, mid, jnp.where(lane == hd + 2, lo, gx)))
        kt[...] = ka_ref[head].astype(F32).T.astype(BF16)
        fill_band(band, rev_ref[head])
        gband[...] = jnp.zeros_like(gband)
        dq[...] = jnp.zeros_like(dq)

        def block(step, carry):
            slot = head * blocks + step
            for at, what in events.items():
                @pl.when(slot == at)
                def _():
                    for stage, k in what:
                        stage(k)
            k0 = pl.multiple_of(step * QB, QB)
            key = ka_ref[head, pl.ds(k0, QB), :]
            value = va_ref[head, pl.ds(k0, QB), :]
            ktb = kt[:, pl.ds(k0, QB)]
            dv = jnp.zeros((QB, 128), F32)
            dk = jnp.zeros((QB, 128), F32)
            for c in range(seq // KC):
                cols = slice(c * KC, (c + 1) * KC)
                off = pl.ds(pl.multiple_of(seq - k0 + c * KC, KC), KC)
                qc = qa_ref[head, cols, :]
                dc = da[cols, :]
                p = jnp.exp(dot(key, qc, NT) + band[:, off])
                ds = p * dot(value, dc, NT)
                gband[:, off] += ds
                db = ds.astype(BF16)
                dv += dot(p.astype(BF16), dc)
                dk += dot(db, qc)
                dq[:, cols] += dot(ktb, db)
            grads[head, pl.ds(k0, QB), hd:2 * hd] = dk[:, :hd].astype(BF16)
            grads[head, pl.ds(k0, QB), 2 * hd:3 * hd] = dv[:, :hd].astype(BF16)
            return carry

        lax.fori_loop(0, blocks, block, 0)
        grads[head, :, 0:hd] = (dq[...] * (hd ** -0.5)).T[:, :hd].astype(BF16)
        acc = gband[0:8, :]
        for g in range(1, QB // 8):
            acc = acc + pltpu.roll(gband[8 * g:8 * g + 8, :], span - 8 * g, 1)
        sub = lax.broadcasted_iota(jnp.int32, (8, span), 0)
        for bit in (1, 2, 4):
            acc = jnp.where((sub & bit) != 0, pltpu.roll(acc, span - bit, 1), acc)
        grev_ref[head] = jnp.sum(acc, axis=0, keepdims=True)
        made = dot(nt_ref[...], grads[head]).astype(BF16)
        for h in range(heads):
            @pl.when(head == h)
            def _():
                works[3 + h][0:width, :] = made
                leave(3 + h)
        return carry

    lax.fori_loop(0, heads, head_body, 0)

    def partial(who, c):
        part = spot(who, c)
        total = dot(grads[0, part, :], w3_ref[0], NT)
        for h in range(1, heads):
            total = total + dot(grads[h, part, :], w3_ref[h], NT)
        return total

    def over(i, c):
        return send(away.at[i, pl.ds(c * size, size)], near_land.at[i, pl.ds(c * size, size)], rnear.at[i, c], {"tensor": near})

    def across(c):
        return send(out_far.at[pl.ds(c * size, size)], far_land.at[pl.ds(c * size, size)], rfar.at[c], {"tensor": far})

    for c in range(CHUNKS):
        away[0, pl.ds(c * size, size), :] = partial(diag, c).astype(BF16)
        over(0, c).start()
    last = 2 + heads
    for c in range(CHUNKS):
        part = pl.ds(c * size, size)
        value = partial(far, c)
        over(0, c).wait_recv()
        out_far[part, :] = (value + near_land[0, part, :].astype(F32)).astype(BF16)
        across(c).start()
        if c == 1:
            stage_d4(4)
            stage_d1(last)
    for c in range(CHUNKS):
        away[1, pl.ds(c * size, size), :] = partial(near, c).astype(BF16)
        over(1, c).start()
    stage_d2(2)
    stage_d4(1)
    for c in range(CHUNKS):
        part = pl.ds(c * size, size)
        y_ref[part, :] = partial(me, c)
    stage_d2(last)
    for c in range(CHUNKS):
        over(1, c).wait_recv()
        part = pl.ds(c * size, size)
        y_ref[part, :] += near_land[1, part, :].astype(F32)
    stage_d3(2)
    stage_d3(last)
    for c in range(CHUNKS):
        part = pl.ds(c * size, size)
        across(c).wait_recv()
        y_ref[part, :] += far_land[part, :].astype(F32)
    stage_d4(last)
    stage_d4(2)
    to_near.wait_send()
    for copy in to_far + passed:
        copy.wait_send()
    for k in range(3):
        first(k, 0).wait_send()
        first(k, 1).wait_send()
        second(k).wait_send()
    for k in range(count):
        back(k).wait_send()
        for j in range(1, outer):
            spread(k, j).wait_send()
            collect(k, j).wait_send()
        emit(k).wait()
    for c in range(CHUNKS):
        over(0, c).wait_send()
        over(1, c).wait_send()
        across(c).wait_send()


def backward(length, grad_rows, w_out, rev, mixed, qa, ka, va, normed_t, w_heads, gates, ups, downs, n, collective_id):
    heads, seq, _ = qa.shape
    span = rev.shape[-1]
    rows, width = grad_rows.shape
    ff = downs[0].shape[0]
    hd = mixed.shape[1] // heads
    rows_pad = -(-width // (16 * n)) * 16 * n
    outer = n // 2
    count = 3 + heads
    vmem = pl.BlockSpec(memory_space=pltpu.VMEM)
    away = pl.BlockSpec(memory_space=pl.ANY)
    dma = pltpu.SemaphoreType.DMA
    shapes = [(width, ff), (width, ff), (ff, width)]
    widths = [ff, ff, width] + [3 * hd] * heads
    heights = [width, width, ff + w_out.shape[0]] + [width] * heads
    buffer = lambda *shape: pltpu.VMEM(shape, BF16)
    half = rows_pad // 2
    scratch = [
        buffer(seq, width), buffer(seq, heads * hd), pltpu.VMEM((QB, span), F32), pltpu.VMEM((QB, span), F32),
        buffer(seq, 128), buffer(128, seq), pltpu.VMEM((128, seq), F32), buffer(heads, seq, 3 * hd),
    ]
    scratch += [buffer(*s) for s in shapes] + [buffer(2, *s) for s in shapes] + [buffer(*s) for s in shapes]
    scratch += [buffer(rows_pad, w) for w in widths] + [buffer(half, w) for w in widths] * 2
    scratch += [buffer(outer - 1, half // outer, w) for w in widths]
    scratch += [buffer(2, rows, width), buffer(rows, width), buffer(2, rows, width), buffer(rows, width)]
    scratch += [dma((2,)), dma((CHUNKS, 2)), dma((CHUNKS, 2)), dma((3, 2)), dma((3, 2, 2)), dma((3, 2)),
                dma((count, 2)), dma((count, outer - 1, 2)), dma((count, outer - 1, 2)), dma((count, 2)), dma((count,)),
                dma((2, CHUNKS, 2)), dma((CHUNKS, 2))]
    results = pl.pallas_call(
        functools.partial(backward_kernel, (heads, rows_pad, ff)),
        out_shape=(jax.ShapeDtypeStruct((rows, width), F32), jax.ShapeDtypeStruct((heads, 1, span), F32))
        + tuple(jax.ShapeDtypeStruct((h, w), BF16) for h, w in zip(heights, widths)),
        in_specs=[pl.BlockSpec(memory_space=pltpu.SMEM)] + [vmem] * 9 + [away] * 12,
        out_specs=(vmem, vmem) + (away,) * count,
        scratch_shapes=scratch,
        compiler_params=pltpu.CompilerParams(collective_id=collective_id, has_side_effects=True, vmem_limit_bytes=62 << 20),
        name="backward",
    )(length, grad_rows, w_out, rev.reshape(heads, 1, span), mixed, qa, ka, va, normed_t, w_heads, *gates, *ups, *downs)
    return results[0], results[1].reshape(heads, span), results[2:]


def on_device(
    inputs,
    teacher,
    lengths,
    buckets,
    gain_attn,
    w_query,
    w_key,
    w_value,
    w_out,
    bias_table,
    gain_ff,
    w_gate,
    w_up,
    w_down,
):
    row_count, model_width = inputs.shape
    group_size = lax.axis_size("tensor")
    dp_size = lax.axis_size("dp")
    seq_len = buckets.shape[0] // 2
    local_width = w_query.shape[1]
    heads_here = bias_table.shape[1]
    ff_width = w_gate.shape[1]
    my_first = lax.axis_index("tensor") * row_count
    keep_mine = (my_first + lax.iota(jnp.int32, row_count) < lengths[0]).astype(F32)[:, None]
    reversed_buckets = jnp.concatenate([buckets[:1], jnp.flip(buckets[1:])])
    _, relative = bucket_rows(buckets, bias_table)
    one_hot, backward_relative = bucket_rows(reversed_buckets, bias_table)
    gain_a = gain_attn.astype(F32)
    gain_f = gain_ff.astype(F32)
    source = inputs.astype(F32)
    normed = row_norm(source, gain_a).astype(BF16)
    head_dim = local_width // heads_here
    by_head = lambda w: w.reshape(model_width, heads_here, 1, head_dim)
    w_joint = jnp.concatenate([by_head(w_query), by_head(w_key), by_head(w_value)], axis=2)
    w_heads = jnp.swapaxes(w_joint.reshape(model_width, heads_here, 3 * head_dim), 0, 1)
    w_joint = w_joint.reshape(model_width, 3 * local_width)
    normed_all, joint = gather_project(normed, w_joint, lengths, NN, False, 1)
    normed_all, joint, w_gate, w_up, w_down = lax.optimization_barrier((normed_all, joint, w_gate, w_up, w_down))

    near_pairs = [(i, i ^ 1) for i in range(group_size)]
    far_pairs = [(i, i ^ 2) for i in range(group_size)]
    near_of = lambda value: lax.ppermute(value, "tensor", near_pairs)
    far_of = lambda value: lax.ppermute(value, "tensor", far_pairs)
    w_pair = jnp.concatenate([w_gate, w_up], axis=1)
    pairs = [w_pair, near_of(w_pair), far_of(w_pair)]
    downs = [w_down, near_of(w_down), far_of(w_down)]
    pairs.append(near_of(pairs[2]))
    downs.append(near_of(downs[2]))

    mixed_parts, query_aug, key_aug, value_aug = attend(lengths, relative, joint, heads_here)
    middle = source + project_scatter(mixed_parts, w_out, NN, 2)
    normed_ff = row_norm(middle, gain_f).astype(BF16)
    gates, ups, hiddens = [], [], []
    output = middle
    for pair, down in zip(pairs, downs):
        paired = dot(normed_ff, pair)
        gates.append(paired[:, :ff_width])
        ups.append(paired[:, ff_width:])
        hiddens.append(geglu_mask(gates[-1], ups[-1], keep_mine).astype(BF16))
        output = output + dot(hiddens[-1], down)
    activations = output.astype(BF16)
    cotangent = keep_mine * (output - teacher.astype(F32))
    loss_part = jnp.sum(cotangent * cotangent)
    count_part = jnp.sum(keep_mine)
    grad_ff_rows = cotangent.astype(BF16)
    grad_normed_ff = 0.0
    down_grads, gate_grads, up_grads = [], [], []
    for pair, down, gate, up, hidden in zip(pairs, downs, gates, ups, hiddens):
        grad_hidden = dot(grad_ff_rows, down, NT)
        _, geglu_back = jax.vjp(lambda g, u: geglu_mask(g, u, keep_mine), gate, up)
        grad_gate_rows, grad_up_rows = (g.astype(BF16) for g in geglu_back(grad_hidden))
        grad_pair = jnp.concatenate([grad_gate_rows, grad_up_rows], axis=1)
        grad_normed_ff = grad_normed_ff + dot(grad_pair, pair, NT)
        down_grads.append(dot(hidden, grad_ff_rows, TN).astype(BF16))
        gate_grads.append(dot(normed_ff, grad_gate_rows, TN).astype(BF16))
        up_grads.append(dot(normed_ff, grad_up_rows, TN).astype(BF16))
    _, norm_back_ff = jax.vjp(row_norm, middle, gain_f)
    grad_middle_part, grad_gain_ff = norm_back_ff(grad_normed_ff)
    grad_middle = cotangent + grad_middle_part

    grad_normed, grad_relative, sums = backward(
        lengths, grad_middle.astype(BF16), w_out, backward_relative, mixed_parts, query_aug, key_aug, value_aug,
        normed_all.T, w_heads, gate_grads, up_grads, down_grads, dp_size, 3,
    )
    grad_table = lax.dot_general(one_hot, grad_relative, contract_table, precision=highest)
    _, norm_back_attn = jax.vjp(row_norm, source, gain_a)
    grad_source_part, grad_gain_attn = norm_back_attn(grad_normed)
    grad_source = grad_middle + grad_source_part

    gain_rows = model_width // 128
    scalars = jnp.zeros((8, 128), F32).at[0, 0].set(loss_part).at[0, 1].set(count_part)
    table_row = jnp.zeros((8, 128), F32).at[7, : grad_table.size].set(grad_table.reshape(-1))
    small = jnp.concatenate(
        [grad_gain_attn.reshape(gain_rows, 128), grad_gain_ff.reshape(gain_rows, 128), scalars, table_row]
    )
    small = jnp.pad(small, ((small.shape[0] % 8, 0), (0, 0)))
    first = small.shape[0] - 16 - 2 * gain_rows
    (small,) = reduce_all([], small, dp_size, 5)
    grad_gate, grad_up, tall = sums[:3]
    by_kind = lambda i: jnp.concatenate([g[:, i * head_dim : (i + 1) * head_dim] for g in sums[3:]], axis=1)
    small = small[first:]
    loss_total, count_total = small[2 * gain_rows, 0], small[2 * gain_rows, 1]
    grad_table = small[-1, : grad_table.size].reshape(grad_table.shape)
    factor = 2.0 / (count_total * model_width)
    scaled = lambda value: value.astype(F32) * factor
    return (
        activations,
        loss_total / (count_total * model_width),
        grad_source * factor,
        small[:gain_rows].reshape(-1) * factor,
        scaled(by_kind(0)),
        scaled(by_kind(1)),
        scaled(by_kind(2)),
        scaled(tall[ff_width:]),
        grad_table * factor,
        small[gain_rows : 2 * gain_rows].reshape(-1) * factor,
        scaled(grad_gate),
        scaled(grad_up),
        scaled(tall[:ff_width]),
    )


def solution(mesh):
    in_specs = (
        P(("dp", "tensor"), None),
        P(("dp", "tensor"), None),
        P("dp"),
        P(),
        P(),
        P(None, "tensor"),
        P(None, "tensor"),
        P(None, "tensor"),
        P("tensor", None),
        P(None, "tensor"),
        P(),
        P(None, "tensor"),
        P(None, "tensor"),
        P("tensor", None),
    )
    out_specs = (
        P(("dp", "tensor"), None),
        P(),
        P(("dp", "tensor"), None),
        P(),
        P(None, "tensor"),
        P(None, "tensor"),
        P(None, "tensor"),
        P("tensor", None),
        P(None, "tensor"),
        P(),
        P(None, "tensor"),
        P(None, "tensor"),
        P("tensor", None),
    )
    return jax.shard_map(
        on_device, mesh=mesh, in_specs=in_specs, out_specs=out_specs, check_vma=False
    )
```
